128 devices in a mesh: scan: 4 (over x_lo, core), pix: 32 (over y, x_hi, z).
Axes of the slice: x: 4 (x_hi: 2, x_lo: 2; x = x_hi * 2 + x_lo), y: 4, z: 4, core: 2. Of those that a mesh axis runs over, the one named last changes fastest.
Arguments:
- raw_frames: float32 [6144, 128, 128], P(('scan', 'pix')), may hold values from 0.2 to 5
- gain_map: float32 [128, 128], replicated, may hold values from 0.5 to 1.5
- coupling: float32 [128, 128], replicated, may hold values from 0.05 to 0.25
- factor_w: float32 [6144, 256], P(('scan', 'pix')), may hold values from 0.01 to 0.25
- factor_h: float32 [256, 16384], P('scan', 'pix'), may hold values from 0.01 to 0.25
Outputs:
- w_factor: float32 [6144, 256], P(('scan', 'pix'))
- h_factor: float32 [256, 16384], P('scan', 'pix')
The draws below stay inside these ranges and needn't reach their ends.
All inputs are finite; a program needn't handle non-finite values.
Results may differ from the reference program's by a relative error of at most 0.0003.
Values may be sent and summed in bfloat16 or wider, within the bound.
A program may use at most 64 MiB of HBM per device.

```python
import math
import jax
import jax.numpy as jnp
from jax import lax

FRAME = 128
RANK = 256
SWEEPS = 4
ITERS = 2
FR_DEV = 48
FRAMES = 6144
PIXELS = 16384
N_SCAN = 4
N_PIX = 32


def shard_levels(rng, extent, shards, smallest, top_value):
    level = 1.0
    for position, shards_of in shards:
        draws = jax.random.uniform(jax.random.fold_in(jax.random.fold_in(rng, 6), position), (shards_of,), jnp.float32, smallest / len(shards), top_value / len(shards))
        level = level * jnp.repeat(jnp.exp(draws), extent[position] // shards_of).reshape((-1,) + (1,) * (len(extent) - 1 - position))
    return level


def setup_inputs(seed: int = 0) -> dict:
    streams_of = jax.random.split(jax.random.key(seed), 6)
    raw_frames = jnp.clip(jnp.exp(math.log(5.0) - 3.218876 * jax.random.uniform(streams_of[0], (FRAMES, FRAME, FRAME), jnp.float32) ** shard_levels(streams_of[0], (FRAMES, FRAME, FRAME), ((0, 128),), -0.2, 0.2)), 0.2, 5.0)
    gain_map = jnp.clip(1.0 + 0.1 * jax.random.normal(streams_of[1], (FRAME, FRAME), jnp.float32), 0.5, 1.5)
    coupling = jnp.clip(jnp.exp(jax.random.uniform(streams_of[2], (FRAME, FRAME), jnp.float32, math.log(0.05), math.log(0.25))), 0.05, 0.25)
    factor_w = jnp.clip(jnp.exp(math.log(0.25) - 3.218876 * jax.random.uniform(streams_of[3], (FRAMES, RANK), jnp.float32) ** shard_levels(streams_of[3], (FRAMES, RANK), ((0, 128),), -0.2, 0.2)), 0.01, 0.25)
    factor_h = jnp.clip(jnp.exp(math.log(0.25) - 3.218876 * jax.random.uniform(streams_of[4], (RANK, PIXELS), jnp.float32) ** shard_levels(streams_of[4], (RANK, PIXELS), ((0, 4), (1, 32)), -0.2, 0.2)), 0.01, 0.25)
    return dict(raw_frames=raw_frames, gain_map=gain_map, coupling=coupling, factor_w=factor_w, factor_h=factor_h)


def stencil(frames, gain_map, coupling):
    measured = frames * gain_map[None]
    charge = measured
    for sweep in range(SWEEPS):
        padded = jnp.pad(charge, ((0, 0), (1, 1), (1, 1)))
        neighbours = padded[:, 2:, 1:-1] + padded[:, :-2, 1:-1] + padded[:, 1:-1, 2:] + padded[:, 1:-1, :-2]
        charge = (measured + coupling[None] * neighbours) / (1.0 + 4.0 * coupling[None])
    return charge.reshape(frames.shape[0], -1)


def reference(raw_frames, gain_map, coupling, factor_w, factor_h):
    block_rows = FR_DEV * N_PIX
    blocks = raw_frames.reshape(N_SCAN, block_rows, FRAME, FRAME)
    tile_data = lax.map(lambda frames: stencil(frames, gain_map, coupling), blocks)
    w_blocks = factor_w.reshape(N_SCAN, block_rows, RANK)
    h_full = factor_h
    for rounds in range(ITERS):
        h_round = h_full.astype(jnp.bfloat16)
        h_sums = jnp.sum(h_round.astype(jnp.float32), axis=1)

        def w_update(pair):
            values, w_block = pair
            w_round = w_block.astype(jnp.bfloat16)
            product = jnp.dot(w_round, h_round, preferred_element_type=jnp.float32)
            count_ratio = (values / product).astype(jnp.bfloat16)
            numerator = jnp.dot(count_ratio, h_round.T, preferred_element_type=jnp.float32)
            return w_block * numerator / h_sums

        w_blocks = lax.map(w_update, (tile_data, w_blocks))
        w_round_all = w_blocks.astype(jnp.bfloat16)
        w_sums = jnp.sum(w_round_all.astype(jnp.float32), axis=(0, 1))

        def h_term(pair):
            values, w_round = pair
            product = jnp.dot(w_round, h_round, preferred_element_type=jnp.float32)
            count_ratio = (values / product).astype(jnp.bfloat16)
            return lax.dot_general(w_round, count_ratio, (((0,), (0,)), ((), ())), preferred_element_type=jnp.float32)

        numerator_h = jnp.sum(lax.map(h_term, (tile_data, w_round_all)), axis=0)
        h_full = h_full * numerator_h / w_sums[:, None]
    return w_blocks.reshape(N_SCAN * block_rows, RANK), h_full
```

```python
import functools

import jax
import jax.numpy as jnp
from jax import lax
from jax.experimental import pallas as pl
from jax.experimental.pallas import tpu as pltpu
from jax.sharding import PartitionSpec as P

SWEEPS = 4
ITERS = 2
FRAME = 128
LANES = 128
EXTENTS = (4, 2, 4)
GROUP = 16
DATA = jnp.float32
SUMS = 8
CHUNK = 4

MESH = pl.DeviceIdType.MESH
F32 = jnp.float32
BF16 = jnp.bfloat16


def kernel(
    n_scan,
    n_pix,
    raw_ref,
    gain_ref,
    couple_ref,
    w_ref,
    h_ref,
    w_out,
    h_out,
    raw_v,
    maps,
    charge,
    tile,
    w_all,
    w_now,
    num_send,
    num_recv,
    h_all,
    h_now,
    ratio,
    numh_send,
    numh_recv,
    raw_sem,
    data_sems,
    own_sem,
    w_sems,
    num_sems,
    h_sems,
    numh_sems,
):
    rows = w_ref.shape[0]
    rank = w_ref.shape[1]
    comps = h_ref.shape[0]
    pixels = h_ref.shape[1]
    block = FRAME // n_pix
    groups = rows // GROUP
    scan = lax.axis_index("scan")
    pix = lax.axis_index("pix")
    ey, ex, ez = EXTENTS
    my, mx, mz = pix // (ex * ez), (pix // ez) % ex, pix % ez

    def ahead(slot):
        dy, dx, dz = slot // (ex * ez), (slot // ez) % ex, slot % ez
        return (((my + dy) % ey) * ex + (mx + dx) % ex) * ez + (mz + dz) % ez

    def behind(slot):
        dy, dx, dz = slot // (ex * ez), (slot // ez) % ex, slot % ez
        return (((my + ey - dy) % ey) * ex + (mx + ex - dx) % ex) * ez + (mz + ez - dz) % ez

    def remote(src, dst, sems, to_scan, to_pix):
        return pltpu.make_async_remote_copy(
            src_ref=src,
            dst_ref=dst,
            send_sem=sems.at[0],
            recv_sem=sems.at[1],
            device_id=(to_scan, to_pix),
            device_id_type=MESH,
        )

    def drain(ref, sem):
        pltpu.make_async_copy(ref, ref, sem).wait()

    for g in range(groups):
        pltpu.make_async_copy(
            raw_ref.at[pl.ds(g * GROUP * FRAME, GROUP * FRAME)], raw_v.at[g], raw_sem.at[g]
        ).start()

    barrier = pltpu.get_barrier_semaphore()

    def greet(slot, carry):
        pl.semaphore_signal(
            barrier, inc=1, device_id=(scan, ahead(slot)), device_id_type=MESH
        )
        return carry

    lax.fori_loop(1, n_pix, greet, 0)
    for j in range(1, n_scan):
        pl.semaphore_signal(
            barrier, inc=1, device_id=((scan + j) % n_scan, pix), device_id_type=MESH
        )

    pad = maps.shape[1] - FRAME
    coupling = couple_ref[...]
    inverse = 1.0 / (1.0 + 4.0 * coupling)
    gain = gain_ref[...]
    zero_rows = jnp.zeros((pad // 2, LANES), F32)
    for i, value in enumerate((gain, gain * inverse, coupling * inverse)):
        maps[i, pl.ds(0, pad // 2), :] = zero_rows
        maps[i, pl.ds(pad // 2, FRAME), :] = value
        maps[i, pl.ds(pad // 2 + FRAME, pad // 2), :] = zero_rows

    w_now[...] = w_ref[...]
    h_now[...] = h_ref[...]
    w_all[0, 0] = w_ref[...].astype(BF16)
    my_rows = pl.ds(pl.multiple_of(scan * comps, comps), comps)
    h_all[0, my_rows, :] = h_ref[...].astype(BF16)

    pl.semaphore_wait(barrier, n_pix - 1 + n_scan - 1)

    def send_w(step):
        def go(slot, carry):
            remote(
                w_all.at[step, 0], w_all.at[step, slot], w_sems.at[step], scan, ahead(slot)
            ).start()
            return carry

        lax.fori_loop(1, n_pix, go, 0)

    def send_h(step):
        for j in range(1, n_scan):
            remote(
                h_all.at[step, my_rows],
                h_all.at[step, my_rows],
                h_sems.at[step],
                (scan + j) % n_scan,
                pix,
            ).start()

    def wait_w(step, which):
        drain(w_all.at[step, pl.ds(1, n_pix - 1)], w_sems.at[step, which])

    def wait_h(step, which):
        drain(h_all.at[step, pl.ds(0, comps * (n_scan - 1))], h_sems.at[step, which])

    send_h(0)
    send_w(0)

    lane = lax.broadcasted_iota(jnp.int32, (GROUP, LANES), 1)
    first, last = lane == 0, lane == LANES - 1
    half = pad // 2

    def correct(g):
        def map_row(i, r):
            return jnp.broadcast_to(maps[i, pl.ds(r, 1), :], (GROUP, LANES))

        def step(t, carry):
            older, mids, scaled = carry
            raw = raw_v[g, pl.ds(t % FRAME, GROUP, stride=FRAME), :]
            fresh = raw * map_row(0, t + half)
            new_older, new_mids = [], []
            new_scaled = [raw * map_row(1, t + half)] + list(scaled[:-1])
            for s in range(SWEEPS):
                up, mid = older[s], mids[s]
                left = jnp.where(first, 0.0, pltpu.roll(mid, 1, 1))
                right = jnp.where(last, 0.0, pltpu.roll(mid, LANES - 1, 1))
                new_older.append(mid)
                new_mids.append(fresh)
                fresh = scaled[s] + map_row(2, t + half - 1 - s) * (
                    (up + fresh) + (left + right)
                )
            charge[t, pl.ds(g * GROUP, GROUP), :] = fresh.astype(charge.dtype)
            return tuple(new_older), tuple(new_mids), tuple(new_scaled)

        zero = maps[0, pl.ds(0, GROUP), :]
        zeros = (zero,) * SWEEPS
        lax.fori_loop(0, FRAME + SWEEPS, step, (zeros, zeros, zeros))

    def block_of(device):
        return pl.ds(SWEEPS + device * block, block)

    for g in range(groups):
        pltpu.make_async_copy(
            raw_ref.at[pl.ds(g * GROUP * FRAME, GROUP * FRAME)], raw_v.at[g], raw_sem.at[g]
        ).wait()
        correct(g)
        frames = pl.ds(g * GROUP, GROUP)
        pltpu.make_async_copy(
            charge.at[block_of(pix), frames], tile.at[0, :, frames], own_sem.at[g]
        ).start()

        def go(slot, carry):
            to = ahead(slot)
            remote(
                charge.at[block_of(to), frames],
                tile.at[slot, :, frames],
                data_sems.at[g],
                scan,
                to,
            ).start()
            return carry

        lax.fori_loop(1, n_pix, go, 0)

    wait_h(0, 1)
    wait_w(0, 1)
    for g in range(groups):
        frames = pl.ds(g * GROUP, GROUP)
        pltpu.make_async_copy(
            charge.at[block_of(pix), frames], tile.at[0, :, frames], own_sem.at[g]
        ).wait()
        drain(tile.at[pl.ds(1, n_pix - 1), :, frames], data_sems.at[g, 1])

    steps = n_pix // CHUNK
    size = CHUNK * rows

    def ratios(step_w, step_h, c):
        slots = pl.ds(c * CHUNK, CHUNK)
        w = w_all[step_w, slots].reshape(size, rank)
        product = jnp.dot(w, h_all[step_h], preferred_element_type=F32)
        parts = []
        for k in range(block):
            data = tile[slots, k].reshape(size, LANES).astype(F32)
            parts.append((data / product[:, k * LANES : (k + 1) * LANES]).astype(BF16))
        return w, jnp.concatenate(parts, axis=1)

    for it in range(ITERS):
        if it > 0:
            wait_h(it, 1)
            drain(num_send.at[pl.ds(1, n_pix - 1)], num_sems.at[it - 1, 0])
        sums = lax.dot_general(
            jnp.ones((SUMS, pixels), BF16),
            h_all[it],
            (((1,), (1,)), ((), ())),
            preferred_element_type=F32,
        )

        def numerators(c, carry, skip=0):
            _, count_ratio = ratios(it, it, c)
            part = lax.dot_general(
                count_ratio, h_all[it], (((1,), (1,)), ((), ())), preferred_element_type=F32
            )
            slots = pl.ds(c * CHUNK, CHUNK)
            num_send[slots, pl.ds(0, rows), :] = part.reshape(CHUNK, rows, rank)
            num_send[slots, pl.ds(rows, SUMS), :] = jnp.broadcast_to(
                sums[None], (CHUNK, SUMS, rank)
            )

            def go(slot, carry):
                remote(
                    num_send.at[slot], num_recv.at[it, slot], num_sems.at[it], scan, behind(slot)
                ).start()
                return carry

            return lax.fori_loop(c * CHUNK + skip, (c + 1) * CHUNK, go, carry)

        numerators(0, 0, skip=1)
        lax.fori_loop(1, steps, numerators, 0)
        drain(num_recv.at[it, pl.ds(1, n_pix - 1)], num_sems.at[it, 1])

        def add(slot, total):
            return total + num_recv[it, slot]

        total = lax.fori_loop(1, n_pix, add, num_send[0])
        w_new = w_now[...] * total[:rows] / total[rows : rows + 1]
        if it == ITERS - 1:
            w_out[...] = w_new
        w_now[...] = w_new
        w_all[it + 1, 0] = w_new.astype(BF16)
        send_w(it + 1)
        wait_w(it + 1, 1)

        def second(c, carry):
            _, count_ratio = ratios(it + 1, it, c)
            ratio[pl.ds(c * size, size), pl.ds(0, pixels)] = count_ratio
            return carry

        ratio[:, pl.ds(pixels, LANES)] = jnp.ones((n_pix * rows, LANES), BF16)
        lax.fori_loop(0, steps, second, 0)
        if it > 0:
            drain(numh_send.at[pl.ds(0, comps * (n_scan - 1))], numh_sems.at[it - 1, 0])
        numh_send[...] = lax.dot_general(
            w_all[it + 1].reshape(n_pix * rows, rank),
            ratio[...],
            (((0,), (0,)), ((), ())),
            preferred_element_type=F32,
        )
        for j in range(1, n_scan):
            to = (scan + j) % n_scan
            remote(
                numh_send.at[pl.ds(pl.multiple_of(to * comps, comps), comps)],
                numh_recv.at[it, j - 1],
                numh_sems.at[it],
                to,
                pix,
            ).start()
        drain(numh_recv.at[it], numh_sems.at[it, 1])
        total_h = numh_send[my_rows, :]
        for j in range(n_scan - 1):
            total_h = total_h + numh_recv[it, j]
        w_sum = total_h[:, pixels:]
        for k in range(block):
            columns = slice(k * LANES, (k + 1) * LANES)
            h_new = h_now[:, columns] * total_h[:, columns] / w_sum
            h_now[:, columns] = h_new
            if it == ITERS - 1:
                h_out[:, columns] = h_new
        if it < ITERS - 1:
            h_all[it + 1, my_rows, :] = h_now[...].astype(BF16)
            send_h(it + 1)

    for g in range(groups):
        frames = pl.ds(g * GROUP, GROUP)
        drain(tile.at[pl.ds(1, n_pix - 1), :, frames], data_sems.at[g, 0])
    for step in range(ITERS + 1):
        wait_w(step, 0)
    for step in range(ITERS):
        wait_h(step, 0)
    drain(num_send.at[pl.ds(1, n_pix - 1)], num_sems.at[ITERS - 1, 0])
    drain(numh_send.at[pl.ds(0, comps * (n_scan - 1))], numh_sems.at[ITERS - 1, 0])


def solution(mesh):
    n_scan, n_pix = mesh.shape["scan"], mesh.shape["pix"]

    def local(raw_frames, gain_map, coupling, factor_w, factor_h):
        frames = raw_frames.shape[0]
        rank = factor_w.shape[1]
        comps, pixels = factor_h.shape
        groups = frames // GROUP
        block = FRAME // n_pix
        vmem = pl.BlockSpec(memory_space=pltpu.VMEM)
        dma = pltpu.SemaphoreType.DMA
        return pl.pallas_call(
            functools.partial(kernel, n_scan, n_pix),
            out_shape=(
                jax.ShapeDtypeStruct(factor_w.shape, F32),
                jax.ShapeDtypeStruct(factor_h.shape, F32),
            ),
            in_specs=[pl.BlockSpec(memory_space=pl.ANY)] + [vmem] * 4,
            out_specs=(vmem, vmem),
            scratch_shapes=[
                pltpu.VMEM((groups, GROUP * FRAME, LANES), F32),
                pltpu.VMEM((3, FRAME + 2 * GROUP, LANES), F32),
                pltpu.VMEM((FRAME + SWEEPS, frames, LANES), DATA),
                pltpu.VMEM((n_pix, block, frames, LANES), DATA),
                pltpu.VMEM((ITERS + 1, n_pix, frames, rank), BF16),
                pltpu.VMEM((frames, rank), F32),
                pltpu.VMEM((n_pix, frames + SUMS, rank), F32),
                pltpu.VMEM((ITERS, n_pix, frames + SUMS, rank), F32),
                pltpu.VMEM((ITERS, rank, pixels), BF16),
                pltpu.VMEM((comps, pixels), F32),
                pltpu.VMEM((n_pix * frames, pixels + LANES), BF16),
                pltpu.VMEM((rank, pixels + LANES), F32),
                pltpu.VMEM((ITERS, n_scan - 1, comps, pixels + LANES), F32),
                dma((groups,)),
                dma((groups, 2)),
                dma((groups,)),
                dma((ITERS + 1, 2)),
                dma((ITERS, 2)),
                dma((ITERS, 2)),
                dma((ITERS, 2)),
            ],
            compiler_params=pltpu.CompilerParams(
                collective_id=0, has_side_effects=True, vmem_limit_bytes=58 * 1024 * 1024
            ),
        )(raw_frames.reshape(frames * FRAME, LANES), gain_map, coupling, factor_w, factor_h)

    return jax.shard_map(
        local,
        mesh=mesh,
        in_specs=(
            P(("scan", "pix"), None, None),
            P(),
            P(),
            P(("scan", "pix"), None),
            P("scan", "pix"),
        ),
        out_specs=(P(("scan", "pix"), None), P("scan", "pix")),
        check_vma=False,
    )
```

```python
import functools

import jax
import jax.numpy as jnp
from jax import lax
from jax.experimental import pallas as pl
from jax.experimental.pallas import tpu as pltpu
from jax.sharding import PartitionSpec as P

SWEEPS = 4
ITERS = 2
FRAME = 128
LANES = 128
EY, EX, EZ = 4, 2, 4
SLOTS = EY * EZ
GROUP = 16
ROWS = 64
DATA = jnp.bfloat16
CHUNK = 4

MESH = pl.DeviceIdType.MESH
F32 = jnp.float32
BF16 = jnp.bfloat16


def kernel(
    n_scan,
    raw_ref,
    gain_ref,
    couple_ref,
    w_ref,
    h_ref,
    w_out,
    h_out,
    raw_v,
    maps,
    scaled,
    field,
    charge,
    tile,
    w_all,
    w_now,
    num_send,
    num_recv,
    h_all,
    h_now,
    hsum_all,
    ratio,
    numh_send,
    numh_recv,
    wsum_all,
    raw_sem,
    data_sems,
    own_sem,
    w_sems,
    num_sems,
    h_sems,
    hsum_sems,
    numh_sems,
    wsum_sems,
):
    rows, rank = w_ref.shape
    comps, pixels = h_ref.shape
    block = pixels // FRAME
    groups = rows // GROUP
    mates = EX * n_scan
    scan = lax.axis_index("scan")
    pix = lax.axis_index("pix")
    my, mx, mz = pix // (EX * EZ), (pix // EZ) % EX, pix % EZ

    def ahead(slot):
        return (my + slot // EZ) % EY, (mz + slot % EZ) % EZ

    def behind(slot):
        return (my + EY - slot // EZ) % EY, (mz + EZ - slot % EZ) % EZ

    def mate(j):
        other = (mx * n_scan + scan + j) % mates
        return other % n_scan, other // n_scan

    def remote(src, dst, sems, to_scan, y, x, z):
        return pltpu.make_async_remote_copy(
            src_ref=src,
            dst_ref=dst,
            send_sem=sems.at[0],
            recv_sem=sems.at[1],
            device_id=(to_scan, (y * EX + x) * EZ + z),
            device_id_type=MESH,
        )

    def to_slot(src, dst, sems, where):
        y, z = where
        return remote(src, dst, sems, scan, y, mx, z)

    def to_mate(src, dst, sems, j):
        to_scan, x = mate(j)
        return remote(src, dst, sems, to_scan, my, x, mz)

    def drain(ref, sem):
        pltpu.make_async_copy(ref, ref, sem).wait()

    def fetch(g):
        return pltpu.make_async_copy(
            raw_ref.at[pl.ds(g * GROUP * FRAME, GROUP * FRAME)], raw_v.at[g], raw_sem.at[g]
        )

    for g in range(groups):
        fetch(g).start()

    barrier = pltpu.get_barrier_semaphore()

    def greet(slot, carry):
        y, z = ahead(slot)
        pl.semaphore_signal(
            barrier, inc=1, device_id=(scan, (y * EX + mx) * EZ + z), device_id_type=MESH
        )
        return carry

    lax.fori_loop(1, SLOTS, greet, 0)
    for j in range(1, mates):
        to_scan, x = mate(j)
        pl.semaphore_signal(
            barrier, inc=1, device_id=(to_scan, (my * EX + x) * EZ + mz), device_id_type=MESH
        )

    coupling = couple_ref[...]
    inverse = 1.0 / (1.0 + 4.0 * coupling)
    gain = gain_ref[...]
    for i, value in enumerate((gain, gain * inverse, coupling * inverse)):
        maps[i] = jnp.broadcast_to(value[:, None, :], (FRAME, 8, LANES))

    w_now[...] = w_ref[...]
    h_now[...] = h_ref[...]
    w_all[0, 0] = w_ref[...].astype(BF16)
    my_comps = pl.ds(pl.multiple_of(scan * comps, comps), comps)
    my_pixels = pl.ds(pl.multiple_of(mx * pixels, pixels), pixels)
    h_all[0, my_comps, my_pixels] = h_ref[...].astype(BF16)

    pl.semaphore_wait(barrier, SLOTS - 1 + mates - 1)

    def send_w(step):
        def go(slot, carry):
            to_slot(
                w_all.at[step, 0], w_all.at[step, slot], w_sems.at[step], ahead(slot)
            ).start()
            return carry

        lax.fori_loop(1, SLOTS, go, 0)

    def send_h(step):
        own = h_all.at[step, my_comps, my_pixels]
        for j in range(1, mates):
            to_mate(own, own, h_sems.at[step], j).start()

    def wait_w(step, which):
        drain(w_all.at[step, pl.ds(1, SLOTS - 1)], w_sems.at[step, which])

    def wait_h(step, which):
        drain(
            h_all.at[step, pl.ds(0, rank * (mates - 1) // mates)], h_sems.at[step, which]
        )

    send_h(0)
    send_w(0)

    lane = lax.broadcasted_iota(jnp.int32, (ROWS, GROUP, LANES), 2)
    first, last = lane == 0, lane == LANES - 1

    for i in range(2):
        edge = jnp.zeros((GROUP, LANES), F32)
        field[i, 0] = edge
        field[i, FRAME + 1] = edge

    def correct(g):
        def map_rows(i, at):
            value = maps[i, pl.ds(at, ROWS)]
            return jnp.concatenate([value] * (GROUP // 8), axis=1)

        def start(c, carry):
            at = c * 8
            for i in range(8):
                raw = raw_v[g, pl.ds(at + i, GROUP, stride=FRAME), :]
                tall = [maps[m, at + i] for m in range(2)]
                gain_row, scaled_row = [
                    jnp.concatenate([v] * (GROUP // 8), axis=0) for v in tall
                ]
                field[0, at + i + 1] = raw * gain_row
                scaled[at + i] = raw * scaled_row
            return carry

        lax.fori_loop(0, FRAME // 8, start, 0)
        for s in range(SWEEPS):

            def sweep(c, carry):
                at = c * ROWS
                rows_in = field[s % 2, pl.ds(at, ROWS + 2)]
                mid = rows_in[1:-1]
                left = jnp.where(first, 0.0, pltpu.roll(mid, 1, 2))
                right = jnp.where(last, 0.0, pltpu.roll(mid, LANES - 1, 2))
                value = scaled[pl.ds(at, ROWS)] + map_rows(2, at) * (
                    (rows_in[:-2] + rows_in[2:]) + (left + right)
                )
                if s == SWEEPS - 1:
                    slabs = ROWS // (EX * EZ * block)
                    charge[pl.ds(c * slabs, slabs), :, :, :, pl.ds(g * GROUP, GROUP), :] = (
                        value.astype(charge.dtype).reshape(slabs, EX, EZ, block, GROUP, LANES)
                    )
                else:
                    field[(s + 1) % 2, pl.ds(at + 1, ROWS)] = value
                return carry

            lax.fori_loop(0, FRAME // ROWS, sweep, 0)

    def own_copy(g):
        frames = pl.ds(g * GROUP, GROUP)
        return pltpu.make_async_copy(
            charge.at[my, :, mz, :, frames], tile.at[0, :, :, frames], own_sem.at[g]
        )

    for g in range(groups):
        fetch(g).wait()
        correct(g)
        own_copy(g).start()
        frames = pl.ds(g * GROUP, GROUP)

        def go(slot, carry):
            y, z = ahead(slot)
            to_slot(
                charge.at[y, :, z, :, frames],
                tile.at[slot, :, :, frames],
                data_sems.at[g],
                (y, z),
            ).start()
            return carry

        lax.fori_loop(1, SLOTS, go, 0)

    steps = SLOTS // CHUNK
    size = CHUNK * rows
    wide = EX * pixels

    def ratios(step_w, step_h, c):
        slots = pl.ds(c * CHUNK, CHUNK)
        w = w_all[step_w, slots].reshape(size, rank)
        product = jnp.dot(w, h_all[step_h], preferred_element_type=F32)
        parts = []
        for x in range(EX):
            for k in range(block):
                at = (x * block + k) * LANES
                data = tile[slots, x, k].reshape(size, LANES).astype(F32)
                parts.append((data / product[:, at : at + LANES]).astype(BF16))
        return jnp.concatenate(parts, axis=1)

    def column_sums(lhs_rows, operand, dims):
        ones = jnp.ones((8, lhs_rows), BF16)
        return lax.dot_general(ones, operand, (dims, ((), ())), preferred_element_type=F32)[:1]

    for it in range(ITERS):
        wait_h(it, 1)
        hsum_all[it, 0] = column_sums(wide, h_all[it], ((1,), (1,)))

        def share(slot, carry):
            to_slot(
                hsum_all.at[it, 0], hsum_all.at[it, slot], hsum_sems.at[it], ahead(slot)
            ).start()
            return carry

        lax.fori_loop(1, SLOTS, share, 0)
        if it == 0:
            wait_w(0, 1)
            for g in range(groups):
                frames = pl.ds(g * GROUP, GROUP)
                own_copy(g).wait()
                drain(tile.at[pl.ds(1, SLOTS - 1), :, :, frames], data_sems.at[g, 1])
        else:
            drain(num_send.at[pl.ds(1, SLOTS - 1)], num_sems.at[it - 1, 0])

        def numerators(c, carry, skip=0):
            part = lax.dot_general(
                ratios(it, it, c),
                h_all[it],
                (((1,), (1,)), ((), ())),
                preferred_element_type=F32,
            )
            num_send[pl.ds(c * CHUNK, CHUNK)] = part.reshape(CHUNK, rows, rank)

            def go(slot, carry):
                to_slot(
                    num_send.at[slot], num_recv.at[it, slot], num_sems.at[it], behind(slot)
                ).start()
                return carry

            return lax.fori_loop(c * CHUNK + skip, (c + 1) * CHUNK, go, carry)

        numerators(0, 0, skip=1)
        lax.fori_loop(1, steps, numerators, 0)
        drain(hsum_all.at[it, pl.ds(1, SLOTS - 1)], hsum_sems.at[it, 1])
        h_sum = hsum_all[it, 0]
        for slot in range(1, SLOTS):
            h_sum = h_sum + hsum_all[it, slot]
        drain(num_recv.at[it, pl.ds(1, SLOTS - 1)], num_sems.at[it, 1])

        def add(slot, total):
            return total + num_recv[it, slot]

        total = lax.fori_loop(1, SLOTS, add, num_send[0])
        w_new = w_now[...] * total / h_sum
        if it == ITERS - 1:
            w_out[...] = w_new
        w_now[...] = w_new
        w_all[it + 1, 0] = w_new.astype(BF16)
        send_w(it + 1)
        wait_w(it + 1, 1)
        wsum_all[it, 0] = column_sums(
            SLOTS * rows, w_all[it + 1].reshape(SLOTS * rows, rank), ((1,), (0,))
        )
        for j in range(1, mates):
            to_mate(wsum_all.at[it, 0], wsum_all.at[it, j], wsum_sems.at[it], j).start()

        def second(c, carry):
            ratio[pl.ds(c * size, size), :] = ratios(it + 1, it, c)
            return carry

        lax.fori_loop(0, steps, second, 0)
        if it > 0:
            drain(numh_send.at[pl.ds(1, mates - 1)], numh_sems.at[it - 1, 0])
        for x in range(EX):
            numh_send[pl.ds(x * n_scan, n_scan)] = lax.dot_general(
                w_all[it + 1].reshape(SLOTS * rows, rank),
                ratio[:, x * pixels : (x + 1) * pixels],
                (((0,), (0,)), ((), ())),
                preferred_element_type=F32,
            ).reshape(n_scan, comps, pixels)
        for j in range(1, mates):
            to_scan, x = mate(j)
            to_mate(
                numh_send.at[x * n_scan + to_scan], numh_recv.at[it, j - 1], numh_sems.at[it], j
            ).start()
        drain(wsum_all.at[it, pl.ds(1, mates - 1)], wsum_sems.at[it, 1])
        w_sum = wsum_all[it, 0]
        for j in range(1, mates):
            w_sum = w_sum + wsum_all[it, j]
        at = lax.broadcasted_iota(jnp.int32, (comps, rank), 1)
        own = lax.broadcasted_iota(jnp.int32, (comps, rank), 0) + scan * comps
        w_sum = jnp.sum(
            jnp.where(at == own, jnp.broadcast_to(w_sum, (comps, rank)), 0.0),
            axis=1,
            keepdims=True,
        )
        drain(numh_recv.at[it], numh_sems.at[it, 1])
        total_h = numh_send[mx * n_scan + scan]
        for j in range(mates - 1):
            total_h = total_h + numh_recv[it, j]
        h_new = h_now[...] * total_h / w_sum
        if it == ITERS - 1:
            h_out[...] = h_new
        else:
            h_now[...] = h_new
            h_all[it + 1, my_comps, my_pixels] = h_new.astype(BF16)
            send_h(it + 1)

    for g in range(groups):
        frames = pl.ds(g * GROUP, GROUP)
        drain(tile.at[pl.ds(1, SLOTS - 1), :, :, frames], data_sems.at[g, 0])
    for step in range(ITERS + 1):
        wait_w(step, 0)
    for step in range(ITERS):
        wait_h(step, 0)
        drain(hsum_all.at[step, pl.ds(1, SLOTS - 1)], hsum_sems.at[step, 0])
        drain(wsum_all.at[step, pl.ds(1, mates - 1)], wsum_sems.at[step, 0])
    drain(num_send.at[pl.ds(1, SLOTS - 1)], num_sems.at[ITERS - 1, 0])
    drain(numh_send.at[pl.ds(1, mates - 1)], numh_sems.at[ITERS - 1, 0])


def solution(mesh):
    n_scan = mesh.shape["scan"]
    mates = EX * n_scan

    def local(raw_frames, gain_map, coupling, factor_w, factor_h):
        frames = raw_frames.shape[0]
        rank = factor_w.shape[1]
        comps, pixels = factor_h.shape
        groups = frames // GROUP
        block = pixels // FRAME
        vmem = pl.BlockSpec(memory_space=pltpu.VMEM)
        dma = pltpu.SemaphoreType.DMA
        return pl.pallas_call(
            functools.partial(kernel, n_scan),
            out_shape=(
                jax.ShapeDtypeStruct(factor_w.shape, F32),
                jax.ShapeDtypeStruct(factor_h.shape, F32),
            ),
            in_specs=[pl.BlockSpec(memory_space=pl.ANY)] + [vmem] * 4,
            out_specs=(vmem, vmem),
            scratch_shapes=[
                pltpu.VMEM((groups, GROUP * FRAME, LANES), F32),
                pltpu.VMEM((3, FRAME, 8, LANES), F32),
                pltpu.VMEM((FRAME, GROUP, LANES), F32),
                pltpu.VMEM((2, FRAME + 2, GROUP, LANES), F32),
                pltpu.VMEM((EY, EX, EZ, block, frames, LANES), DATA),
                pltpu.VMEM((SLOTS, EX, block, frames, LANES), DATA),
                pltpu.VMEM((ITERS + 1, SLOTS, frames, rank), BF16),
                pltpu.VMEM((frames, rank), F32),
                pltpu.VMEM((SLOTS, frames, rank), F32),
                pltpu.VMEM((ITERS, SLOTS, frames, rank), F32),
                pltpu.VMEM((ITERS, rank, EX * pixels), BF16),
                pltpu.VMEM((comps, pixels), F32),
                pltpu.VMEM((ITERS, SLOTS, 1, rank), F32),
                pltpu.VMEM((SLOTS * frames, EX * pixels), BF16),
                pltpu.VMEM((mates, comps, pixels), F32),
                pltpu.VMEM((ITERS, mates - 1, comps, pixels), F32),
                pltpu.VMEM((ITERS, mates, 1, rank), F32),
                dma((groups,)),
                dma((groups, 2)),
                dma((groups,)),
                dma((ITERS + 1, 2)),
                dma((ITERS, 2)),
                dma((ITERS, 2)),
                dma((ITERS, 2)),
                dma((ITERS, 2)),
                dma((ITERS, 2)),
            ],
            compiler_params=pltpu.CompilerParams(
                collective_id=0, has_side_effects=True, vmem_limit_bytes=58 * 1024 * 1024
            ),
        )(raw_frames.reshape(frames * FRAME, LANES), gain_map, coupling, factor_w, factor_h)

    return jax.shard_map(
        local,
        mesh=mesh,
        in_specs=(
            P(("scan", "pix"), None, None),
            P(),
            P(),
            P(("scan", "pix"), None),
            P("scan", "pix"),
        ),
        out_specs=(P(("scan", "pix"), None), P("scan", "pix")),
        check_vma=False,
    )
```

```python
import functools

import jax
import jax.numpy as jnp
from jax import lax
from jax.experimental import pallas as pl
from jax.experimental.pallas import tpu as pltpu
from jax.sharding import PartitionSpec as P

SWEEPS = 4
ITERS = 2
FRAME = 128
LANES = 128
EY, EX, EZ = 4, 2, 4
SLOTS = EY * EZ
GROUP = 16
ROWS = 64
DATA = jnp.bfloat16
CHUNK = 4

MESH = pl.DeviceIdType.MESH
F32 = jnp.float32
BF16 = jnp.bfloat16


def kernel(
    n_scan,
    raw_ref,
    gain_ref,
    couple_ref,
    w_ref,
    h_ref,
    w_out,
    h_out,
    raw_v,
    maps,
    scaled,
    field,
    charge,
    tile,
    w_all,
    w_now,
    gain_v,
    couple_v,
    num_send,
    num_recv,
    h_all,
    h_now,
    hsum_all,
    ratio,
    numh_send,
    pair_recv,
    pair_sum,
    numh_recv,
    wsum_all,
    raw_sem,
    data_sems,
    own_sem,
    w_sems,
    num_sems,
    h_sems,
    hsum_sems,
    pair_sems,
    numh_sems,
    wsum_sems,
    out_sems,
):
    rows, rank = w_ref.shape
    comps, pixels = h_ref.shape
    block = pixels // FRAME
    groups = rows // GROUP
    mates = EX * n_scan
    scan = lax.axis_index("scan")
    pix = lax.axis_index("pix")
    my, mx, mz = pix // (EX * EZ), (pix // EZ) % EX, pix % EZ

    def ahead(slot):
        return (my + slot // EZ) % EY, (mz + slot % EZ) % EZ

    def behind(slot):
        return (my + EY - slot // EZ) % EY, (mz + EZ - slot % EZ) % EZ

    def mate(j):
        other = (mx * n_scan + scan + j) % mates
        return other % n_scan, other // n_scan

    def remote(src, dst, sems, to_scan, y, x, z, part=0):
        return pltpu.make_async_remote_copy(
            src_ref=src,
            dst_ref=dst,
            send_sem=sems.at[0],
            recv_sem=sems.at[1 + part],
            device_id=(to_scan, (y * EX + x) * EZ + z),
            device_id_type=MESH,
        )

    def to_slot(src, dst, sems, where, part=0):
        y, z = where
        return remote(src, dst, sems, scan, y, mx, z, part)

    def to_mate(src, dst, sems, j):
        to_scan, x = mate(j)
        return remote(src, dst, sems, to_scan, my, x, mz)

    def drain(ref, sem):
        pltpu.make_async_copy(ref, ref, sem).wait()

    def fetch(g):
        return pltpu.make_async_copy(
            raw_ref.at[pl.ds(g * GROUP * FRAME, GROUP * FRAME)], raw_v.at[g], raw_sem.at[g]
        )

    small = [
        pltpu.make_async_copy(src, dst, raw_sem.at[groups + i])
        for i, (src, dst) in enumerate(
            ((w_ref, w_now), (h_ref, h_now), (gain_ref, gain_v), (couple_ref, couple_v))
        )
    ]
    for copy in small:
        copy.start()
    for g in range(groups):
        fetch(g).start()

    barrier = pltpu.get_barrier_semaphore()

    def greet(slot, carry):
        y, z = ahead(slot)
        pl.semaphore_signal(
            barrier, inc=1, device_id=(scan, (y * EX + mx) * EZ + z), device_id_type=MESH
        )
        return carry

    lax.fori_loop(1, SLOTS, greet, 0)
    for j in range(1, mates):
        to_scan, x = mate(j)
        pl.semaphore_signal(
            barrier, inc=1, device_id=(to_scan, (my * EX + x) * EZ + mz), device_id_type=MESH
        )

    my_comps = pl.ds(pl.multiple_of(scan * comps, comps), comps)
    my_pixels = pl.ds(pl.multiple_of(mx * pixels, pixels), pixels)
    for copy in small:
        copy.wait()
    w_all[0, 0] = w_now[...].astype(BF16)
    h_all[0, my_comps, my_pixels] = h_now[...].astype(BF16)

    pl.semaphore_wait(barrier, SLOTS - 1 + mates - 1)

    def send_w(step):
        def go(slot, carry):
            to_slot(
                w_all.at[step, 0],
                w_all.at[step, slot],
                w_sems.at[step],
                ahead(slot),
                slot // CHUNK,
            ).start()
            return carry

        lax.fori_loop(1, SLOTS, go, 0)

    def send_h(step):
        own = h_all.at[step, my_comps, my_pixels]
        for j in range(1, mates):
            to_mate(own, own, h_sems.at[step], j).start()

    def part_of(c, skip):
        return pl.ds(c * CHUNK + skip, CHUNK - skip)

    def wait_w(step, c, skip):
        drain(w_all.at[step, part_of(c, skip)], w_sems.at[step, 1 + c])

    def wait_h(step, which):
        drain(
            h_all.at[step, pl.ds(0, rank * (mates - 1) // mates)], h_sems.at[step, which]
        )

    send_h(0)
    send_w(0)

    coupling = couple_v[...]
    inverse = 1.0 / (1.0 + 4.0 * coupling)
    gain = gain_v[...]
    for i, value in enumerate((gain, gain * inverse, coupling * inverse)):
        maps[i] = jnp.broadcast_to(value[:, None, :], (FRAME, 8, LANES))

    lane = lax.broadcasted_iota(jnp.int32, (ROWS, GROUP, LANES), 2)
    first, last = lane == 0, lane == LANES - 1

    for i in range(2):
        edge = jnp.zeros((GROUP, LANES), F32)
        field[i, 0] = edge
        field[i, FRAME + 1] = edge

    def correct(g):
        def map_rows(i, at):
            value = maps[i, pl.ds(at, ROWS)]
            return jnp.concatenate([value] * (GROUP // 8), axis=1)

        def start(c, carry):
            at = c * 8
            for i in range(8):
                raw = raw_v[g, pl.ds(at + i, GROUP, stride=FRAME), :]
                tall = [maps[m, at + i] for m in range(2)]
                gain_row, scaled_row = [
                    jnp.concatenate([v] * (GROUP // 8), axis=0) for v in tall
                ]
                field[0, at + i + 1] = raw * gain_row
                scaled[at + i] = raw * scaled_row
            return carry

        lax.fori_loop(0, FRAME // 8, start, 0)
        for s in range(SWEEPS):

            def sweep(c, carry):
                at = c * ROWS
                rows_in = field[s % 2, pl.ds(at, ROWS + 2)]
                mid = rows_in[1:-1]
                left = jnp.where(first, 0.0, pltpu.roll(mid, 1, 2))
                right = jnp.where(last, 0.0, pltpu.roll(mid, LANES - 1, 2))
                value = scaled[pl.ds(at, ROWS)] + map_rows(2, at) * (
                    (rows_in[:-2] + rows_in[2:]) + (left + right)
                )
                if s == SWEEPS - 1:
                    slabs = ROWS // (EX * EZ * block)
                    charge[pl.ds(c * slabs, slabs), :, :, :, pl.ds(g * GROUP, GROUP), :] = (
                        value.astype(charge.dtype).reshape(slabs, EX, EZ, block, GROUP, LANES)
                    )
                else:
                    field[(s + 1) % 2, pl.ds(at + 1, ROWS)] = value
                return carry

            lax.fori_loop(0, FRAME // ROWS, sweep, 0)

    def own_copy(g):
        frames = pl.ds(g * GROUP, GROUP)
        return pltpu.make_async_copy(
            charge.at[my, :, mz, :, frames], tile.at[0, :, :, frames], own_sem.at[g]
        )

    for g in range(groups):
        fetch(g).wait()
        correct(g)
        own_copy(g).start()
        frames = pl.ds(g * GROUP, GROUP)

        def go(slot, carry):
            y, z = ahead(slot)
            to_slot(
                charge.at[y, :, z, :, frames],
                tile.at[slot, :, :, frames],
                data_sems.at[g],
                (y, z),
                slot // CHUNK,
            ).start()
            return carry

        lax.fori_loop(1, SLOTS, go, 0)

    steps = SLOTS // CHUNK
    size = CHUNK * rows
    cores = n_scan // 2
    low, core = scan // cores, scan % cores
    n_chips = EX * 2

    def pair_copy(it, far, side):
        k = far * 2 + side
        other = (core + 1) % cores
        there = (low + side) % 2 * cores + other
        return remote(
            numh_send.at[far, there],
            pair_recv.at[it, k],
            pair_sems.at[it, k],
            low * cores + other,
            my,
            mx,
            mz,
        )

    def chip_copy(it, far, side):
        k = far * 2 + side
        return remote(
            pair_sum.at[k],
            numh_recv.at[it, k - 1],
            numh_sems.at[it, k],
            (low + side) % 2 * cores + core,
            my,
            (mx + far) % EX,
            mz,
        )
    wide = EX * pixels

    def ratios(step_w, step_h, c):
        slots = pl.ds(c * CHUNK, CHUNK)
        w = w_all[step_w, slots].reshape(size, rank)
        product = jnp.dot(w, h_all[step_h], preferred_element_type=F32)
        parts = []
        for x in range(EX):
            for k in range(block):
                at = (x * block + k) * LANES
                data = tile[slots, x, k].reshape(size, LANES).astype(F32)
                parts.append((data / product[:, at : at + LANES]).astype(BF16))
        return jnp.concatenate(parts, axis=1)

    def column_sums(lhs_rows, operand, dims):
        ones = jnp.ones((8, lhs_rows), BF16)
        return lax.dot_general(ones, operand, (dims, ((), ())), preferred_element_type=F32)[:1]

    for it in range(ITERS):
        wait_h(it, 1)
        hsum_all[it, 0] = column_sums(wide, h_all[it], ((1,), (1,)))

        def share(slot, carry):
            to_slot(
                hsum_all.at[it, 0], hsum_all.at[it, slot], hsum_sems.at[it], ahead(slot)
            ).start()
            return carry

        lax.fori_loop(1, SLOTS, share, 0)
        if it == 0:
            for g in range(groups):
                own_copy(g).wait()
        else:
            drain(num_send.at[pl.ds(1, SLOTS - 1)], num_sems.at[it - 1, 0])

        def numerators(c, carry, skip=0):
            if it == 0:
                wait_w(0, c, skip)
                for g in range(groups):
                    frames = pl.ds(g * GROUP, GROUP)
                    drain(tile.at[part_of(c, skip), :, :, frames], data_sems.at[g, 1 + c])
            part = lax.dot_general(
                ratios(it, it, c),
                h_all[it],
                (((1,), (1,)), ((), ())),
                preferred_element_type=F32,
            )
            num_send[pl.ds(c * CHUNK, CHUNK)] = part.reshape(CHUNK, rows, rank)

            def go(slot, carry):
                to_slot(
                    num_send.at[slot], num_recv.at[it, slot], num_sems.at[it], behind(slot), c
                ).start()
                return carry

            return lax.fori_loop(c * CHUNK + skip, (c + 1) * CHUNK, go, carry)

        numerators(0, 0, skip=1)
        lax.fori_loop(1, steps, numerators, 0)
        drain(hsum_all.at[it, pl.ds(1, SLOTS - 1)], hsum_sems.at[it, 1])
        h_sum = hsum_all[it, 0]
        for slot in range(1, SLOTS):
            h_sum = h_sum + hsum_all[it, slot]

        def add(slot, total):
            return total + num_recv[it, slot]

        total = num_send[0]
        for c in range(steps):
            skip = int(c == 0)
            drain(num_recv.at[it, part_of(c, skip)], num_sems.at[it, 1 + c])
            total = lax.fori_loop(c * CHUNK + skip, (c + 1) * CHUNK, add, total)
        w_new = w_now[...] * total / h_sum
        w_now[...] = w_new
        w_all[it + 1, 0] = w_new.astype(BF16)
        send_w(it + 1)
        if it == ITERS - 1:
            pltpu.make_async_copy(w_now, w_out, out_sems.at[0]).start()

        def second(c, sums, skip=0):
            wait_w(it + 1, c, skip)
            slots = pl.ds(c * CHUNK, CHUNK)
            w = w_all[it + 1, slots].reshape(size, rank)
            ratio[pl.ds(c * size, size), :] = ratios(it + 1, it, c)
            return sums + column_sums(size, w, ((1,), (0,)))

        sums = second(0, jnp.zeros((1, rank), F32), skip=1)
        wsum_all[it, 0] = lax.fori_loop(1, steps, second, sums)
        for j in range(1, mates):
            to_mate(wsum_all.at[it, 0], wsum_all.at[it, j], wsum_sems.at[it], j).start()
        if it > 0:
            for far in range(2):
                for side in range(2):
                    pair_copy(it - 1, far, side).wait_send()
                    if far * 2 + side > 0:
                        chip_copy(it - 1, far, side).wait_send()
        for far in (1, 0):
            x = (mx + far) % EX
            part = lax.dot_general(
                w_all[it + 1].reshape(SLOTS * rows, rank),
                ratio[:, pl.ds(pl.multiple_of(x * pixels, pixels), pixels)],
                (((0,), (0,)), ((), ())),
                preferred_element_type=F32,
            )
            numh_send[far] = part.reshape(n_scan, comps, pixels)
            for side in (1, 0):
                pair_copy(it, far, side).start()
        for far in (1, 0):
            for side in (1, 0):
                k = far * 2 + side
                pair_copy(it, far, side).wait_recv()
                here = (low + side) % 2 * cores + core
                pair_sum[k] = numh_send[far, here] + pair_recv[it, k]
                if k > 0:
                    chip_copy(it, far, side).start()
        drain(wsum_all.at[it, pl.ds(1, mates - 1)], wsum_sems.at[it, 1])
        w_sum = wsum_all[it, 0]
        for j in range(1, mates):
            w_sum = w_sum + wsum_all[it, j]
        at = lax.broadcasted_iota(jnp.int32, (comps, rank), 1)
        own = lax.broadcasted_iota(jnp.int32, (comps, rank), 0) + scan * comps
        w_sum = jnp.sum(
            jnp.where(at == own, jnp.broadcast_to(w_sum, (comps, rank)), 0.0),
            axis=1,
            keepdims=True,
        )
        total_h = pair_sum[0]
        for far, side in ((0, 1), (1, 0), (1, 1)):
            chip_copy(it, far, side).wait_recv()
            total_h = total_h + numh_recv[it, far * 2 + side - 1]
        h_new = h_now[...] * total_h / w_sum
        h_now[...] = h_new
        if it == ITERS - 1:
            pltpu.make_async_copy(h_now, h_out, out_sems.at[1]).start()
        else:
            h_all[it + 1, my_comps, my_pixels] = h_new.astype(BF16)
            send_h(it + 1)

    for g in range(groups):
        frames = pl.ds(g * GROUP, GROUP)
        drain(tile.at[pl.ds(1, SLOTS - 1), :, :, frames], data_sems.at[g, 0])
    for step in range(ITERS + 1):
        drain(w_all.at[step, pl.ds(1, SLOTS - 1)], w_sems.at[step, 0])
    for step in range(ITERS):
        wait_h(step, 0)
        drain(hsum_all.at[step, pl.ds(1, SLOTS - 1)], hsum_sems.at[step, 0])
        drain(wsum_all.at[step, pl.ds(1, mates - 1)], wsum_sems.at[step, 0])
    drain(num_send.at[pl.ds(1, SLOTS - 1)], num_sems.at[ITERS - 1, 0])
    for far in range(2):
        for side in range(2):
            pair_copy(ITERS - 1, far, side).wait_send()
            if far * 2 + side > 0:
                chip_copy(ITERS - 1, far, side).wait_send()
    pltpu.make_async_copy(w_now, w_out, out_sems.at[0]).wait()
    pltpu.make_async_copy(h_now, h_out, out_sems.at[1]).wait()


def solution(mesh):
    n_scan = mesh.shape["scan"]
    mates = EX * n_scan

    def local(raw_frames, gain_map, coupling, factor_w, factor_h):
        frames = raw_frames.shape[0]
        rank = factor_w.shape[1]
        comps, pixels = factor_h.shape
        groups = frames // GROUP
        block = pixels // FRAME
        steps = SLOTS // CHUNK
        hbm = pl.BlockSpec(memory_space=pl.ANY)
        dma = pltpu.SemaphoreType.DMA
        return pl.pallas_call(
            functools.partial(kernel, n_scan),
            out_shape=(
                jax.ShapeDtypeStruct(factor_w.shape, F32),
                jax.ShapeDtypeStruct(factor_h.shape, F32),
            ),
            in_specs=[hbm] * 5,
            out_specs=(hbm, hbm),
            scratch_shapes=[
                pltpu.VMEM((groups, GROUP * FRAME, LANES), F32),
                pltpu.VMEM((3, FRAME, 8, LANES), F32),
                pltpu.VMEM((FRAME, GROUP, LANES), F32),
                pltpu.VMEM((2, FRAME + 2, GROUP, LANES), F32),
                pltpu.VMEM((EY, EX, EZ, block, frames, LANES), DATA),
                pltpu.VMEM((SLOTS, EX, block, frames, LANES), DATA),
                pltpu.VMEM((ITERS + 1, SLOTS, frames, rank), BF16),
                pltpu.VMEM((frames, rank), F32),
                pltpu.VMEM((FRAME, LANES), F32),
                pltpu.VMEM((FRAME, LANES), F32),
                pltpu.VMEM((SLOTS, frames, rank), F32),
                pltpu.VMEM((ITERS, SLOTS, frames, rank), F32),
                pltpu.VMEM((ITERS, rank, EX * pixels), BF16),
                pltpu.VMEM((comps, pixels), F32),
                pltpu.VMEM((ITERS, SLOTS, 1, rank), F32),
                pltpu.VMEM((SLOTS * frames, EX * pixels), BF16),
                pltpu.VMEM((EX, n_scan, comps, pixels), F32),
                pltpu.VMEM((ITERS, mates // 2, comps, pixels), F32),
                pltpu.VMEM((mates // 2, comps, pixels), F32),
                pltpu.VMEM((ITERS, mates // 2 - 1, comps, pixels), F32),
                pltpu.VMEM((ITERS, mates, 1, rank), F32),
                dma((groups + 4,)),
                dma((groups, 1 + steps)),
                dma((groups,)),
                dma((ITERS + 1, 1 + steps)),
                dma((ITERS, 1 + steps)),
                dma((ITERS, 2)),
                dma((ITERS, 2)),
                dma((ITERS, mates // 2, 2)),
                dma((ITERS, mates // 2, 2)),
                dma((ITERS, 2)),
                dma((2,)),
            ],
            compiler_params=pltpu.CompilerParams(
                collective_id=0, has_side_effects=True, vmem_limit_bytes=58 * 1024 * 1024
            ),
        )(raw_frames.reshape(frames * FRAME, LANES), gain_map, coupling, factor_w, factor_h)

    return jax.shard_map(
        local,
        mesh=mesh,
        in_specs=(
            P(("scan", "pix"), None, None),
            P(),
            P(),
            P(("scan", "pix"), None),
            P("scan", "pix"),
        ),
        out_specs=(P(("scan", "pix"), None), P("scan", "pix")),
        check_vma=False,
    )
```

```python
import functools

import jax
import jax.numpy as jnp
from jax import lax
from jax.experimental import pallas as pl
from jax.experimental.pallas import tpu as pltpu
from jax.sharding import PartitionSpec as P

SWEEPS = 4
ITERS = 2
FRAME = 128
LANES = 128
EY, EX, EZ = 4, 2, 4
SLOTS = EY * EZ
GROUP = 16
ROWS = 64
DATA = jnp.bfloat16
PARTS = ((0, 2 * GROUP), (2 * GROUP, GROUP))
UNITS = ((0, 0, SLOTS // 2), (0, SLOTS // 2, SLOTS // 2), (1, 0, SLOTS))
HALF = SLOTS // 2

MESH = pl.DeviceIdType.MESH
F32 = jnp.float32
BF16 = jnp.bfloat16


def kernel(
    n_scan,
    raw_ref,
    gain_ref,
    couple_ref,
    w_ref,
    h_ref,
    w_out,
    h_out,
    raw_v,
    maps,
    scaled,
    field,
    charge,
    tile,
    w_first,
    w_second,
    w_now,
    gain_v,
    couple_v,
    num_send_first,
    num_send_second,
    num_recv_first,
    num_recv_second,
    h_all,
    h_now,
    hsum_all,
    ratio,
    numh_send,
    pair_recv,
    pair_sum,
    numh_recv,
    wsum_all,
    raw_sem,
    data_sems,
    own_sem,
    w_sems,
    num_sems,
    h_sems,
    h_pair_sems,
    hsum_sems,
    pair_sems,
    numh_sems,
    wsum_sems,
    out_sems,
):
    rows, rank = w_ref.shape
    comps, pixels = h_ref.shape
    block = pixels // FRAME
    groups = rows // GROUP
    mates = EX * n_scan
    w_all = (w_first, w_second)
    num_send = (num_send_first, num_send_second)
    num_recv = (num_recv_first, num_recv_second)
    scan = lax.axis_index("scan")
    pix = lax.axis_index("pix")
    my, mx, mz = pix // (EX * EZ), (pix // EZ) % EX, pix % EZ
    cores = n_scan // 2
    low, core = scan // cores, scan % cores
    twin = (core + 1) % cores

    def ahead(slot):
        return (my + slot // EZ) % EY, (mz + slot % EZ) % EZ

    def behind(slot):
        return (my + EY - slot // EZ) % EY, (mz + EZ - slot % EZ) % EZ

    def mate(j):
        other = (mx * n_scan + scan + j) % mates
        return other % n_scan, other // n_scan

    def remote(src, dst, sems, to_scan, y, x, z, part=0):
        return pltpu.make_async_remote_copy(
            src_ref=src,
            dst_ref=dst,
            send_sem=sems.at[0],
            recv_sem=sems.at[1 + part],
            device_id=(to_scan, (y * EX + x) * EZ + z),
            device_id_type=MESH,
        )

    def to_slot(src, dst, sems, where, part=0):
        y, z = where
        return remote(src, dst, sems, scan, y, mx, z, part)

    def to_mate(src, dst, sems, j):
        to_scan, x = mate(j)
        return remote(src, dst, sems, to_scan, my, x, mz)

    def drain(ref, sem):
        pltpu.make_async_copy(ref, ref, sem).wait()

    def fetch(g):
        return pltpu.make_async_copy(
            raw_ref.at[pl.ds(g * GROUP * FRAME, GROUP * FRAME)], raw_v.at[g], raw_sem.at[g]
        )

    small = [
        pltpu.make_async_copy(src, dst, raw_sem.at[groups + i])
        for i, (src, dst) in enumerate(
            ((w_ref, w_now), (h_ref, h_now), (gain_ref, gain_v), (couple_ref, couple_v))
        )
    ]
    for copy in small:
        copy.start()
    for g in range(groups):
        fetch(g).start()

    barrier = pltpu.get_barrier_semaphore()

    def greet(slot, carry):
        y, z = ahead(slot)
        pl.semaphore_signal(
            barrier, inc=1, device_id=(scan, (y * EX + mx) * EZ + z), device_id_type=MESH
        )
        return carry

    lax.fori_loop(1, SLOTS, greet, 0)
    for j in range(1, mates):
        to_scan, x = mate(j)
        pl.semaphore_signal(
            barrier, inc=1, device_id=(to_scan, (my * EX + x) * EZ + mz), device_id_type=MESH
        )

    for copy in small:
        copy.wait()

    def part_rows(p):
        return pl.ds(*PARTS[p])

    def send_w(step, p):
        for copy_slots in ((1, HALF), (HALF, SLOTS)):

            def go(slot, carry):
                to_slot(
                    w_all[p].at[step, 0],
                    w_all[p].at[step, slot],
                    w_sems.at[step, p],
                    ahead(slot),
                    copy_slots[0] // HALF,
                ).start()
                return carry

            lax.fori_loop(*copy_slots, go, 0)

    def halves(u):
        _, start, count = UNITS[u]
        both = ((1, HALF - 1, 0), (HALF, HALF, 1))
        return [h for h in both if start <= h[0] < start + count]

    def wait_w(step, u):
        p = UNITS[u][0]
        for start, count, half in halves(u):
            drain(w_all[p].at[step, pl.ds(start, count)], w_sems.at[step, p, 1 + half])

    def place(far, side, of_core):
        at = (low + side) % 2 * cores + of_core
        return (
            pl.ds(pl.multiple_of(at * comps, comps), comps),
            pl.ds(pl.multiple_of((mx + far) % EX * pixels, pixels), pixels),
        )

    mine = place(0, 0, core)

    def h_chip(step, far, side):
        own = h_all.at[step, mine[0], mine[1]]
        return remote(
            own,
            own,
            h_sems.at[step, far * 2 + side],
            (low + side) % 2 * cores + core,
            my,
            (mx + far) % EX,
            mz,
        )

    def h_pair(step, far, side):
        at = place(far, side, core)
        part = h_all.at[step, at[0], at[1]]
        return remote(
            part, part, h_pair_sems.at[step, far * 2 + side], low * cores + twin, my, mx, mz
        )

    others = ((1, 0), (1, 1), (0, 1))
    every = ((0, 0),) + others

    def send_h(step):
        for far, side in others:
            h_chip(step, far, side).start()
        h_pair(step, 0, 0).start()

    def finish_h(step):
        for far, side in others[::-1]:
            h_chip(step, far, side).wait_recv()
            h_pair(step, far, side).start()
        for far, side in every:
            h_pair(step, far, side).wait_recv()

    for p in range(2):
        w_all[p][0, 0] = w_now[part_rows(p), :].astype(BF16)
    h_all[0, mine[0], mine[1]] = h_now[...].astype(BF16)

    def meet():
        pl.semaphore_wait(barrier, SLOTS - 1 + mates - 1)
        send_h(0)
        for p in range(2):
            send_w(0, p)

    coupling = couple_v[...]
    inverse = 1.0 / (1.0 + 4.0 * coupling)
    gain = gain_v[...]
    for i, value in enumerate((gain, gain * inverse, coupling * inverse)):
        maps[i] = jnp.broadcast_to(value[:, None, :], (FRAME, 8, LANES))

    lane = lax.broadcasted_iota(jnp.int32, (ROWS, GROUP, LANES), 2)
    first, last = lane == 0, lane == LANES - 1

    for i in range(2):
        edge = jnp.zeros((GROUP, LANES), F32)
        field[i, 0] = edge
        field[i, FRAME + 1] = edge

    def correct(g, between=None):
        def map_rows(i, at):
            value = maps[i, pl.ds(at, ROWS)]
            return jnp.concatenate([value] * (GROUP // 8), axis=1)

        def start(c, carry):
            at = c * 8
            for i in range(8):
                raw = raw_v[g, pl.ds(at + i, GROUP, stride=FRAME), :]
                tall = [maps[m, at + i] for m in range(2)]
                gain_row, scaled_row = [
                    jnp.concatenate([v] * (GROUP // 8), axis=0) for v in tall
                ]
                field[0, at + i + 1] = raw * gain_row
                scaled[at + i] = raw * scaled_row
            return carry

        lax.fori_loop(0, FRAME // 8, start, 0)
        for s in range(SWEEPS):

            def sweep(c, carry):
                at = c * ROWS
                rows_in = field[s % 2, pl.ds(at, ROWS + 2)]
                mid = rows_in[1:-1]
                left = jnp.where(first, 0.0, pltpu.roll(mid, 1, 2))
                right = jnp.where(last, 0.0, pltpu.roll(mid, LANES - 1, 2))
                value = scaled[pl.ds(at, ROWS)] + map_rows(2, at) * (
                    (rows_in[:-2] + rows_in[2:]) + (left + right)
                )
                if s == SWEEPS - 1:
                    slabs = ROWS // (EX * EZ * block)
                    charge[pl.ds(c * slabs, slabs), :, :, :, pl.ds(g * GROUP, GROUP), :] = (
                        value.astype(charge.dtype).reshape(slabs, EX, EZ, block, GROUP, LANES)
                    )
                else:
                    field[(s + 1) % 2, pl.ds(at + 1, ROWS)] = value
                return carry

            lax.fori_loop(0, FRAME // ROWS, sweep, 0)
            if s == 1 and between is not None:
                between()

    def own_copy(g):
        frames = pl.ds(g * GROUP, GROUP)
        return pltpu.make_async_copy(
            charge.at[my, :, mz, :, frames], tile.at[0, :, :, frames], own_sem.at[g]
        )

    for g in range(groups):
        fetch(g).wait()
        correct(g, meet if g == 0 else None)
        own_copy(g).start()
        frames = pl.ds(g * GROUP, GROUP)

        for half, (start, stop) in enumerate(((1, HALF), (HALF, SLOTS))):

            def go(slot, carry):
                y, z = ahead(slot)
                to_slot(
                    charge.at[y, :, z, :, frames],
                    tile.at[slot, :, :, frames],
                    data_sems.at[g],
                    (y, z),
                    half,
                ).start()
                return carry

            lax.fori_loop(start, stop, go, 0)

    wide = EX * pixels
    unit_rows = [count * PARTS[p][1] for p, _, count in UNITS]
    unit_start = [sum(unit_rows[:u]) for u in range(len(UNITS))]

    def pair_copy(it, far, side):
        k = far * 2 + side
        there = (low + side) % 2 * cores + twin
        return remote(
            numh_send.at[far, there],
            pair_recv.at[it, k],
            pair_sems.at[it, k],
            low * cores + twin,
            my,
            mx,
            mz,
        )

    def chip_copy(it, far, side):
        k = far * 2 + side
        return remote(
            pair_sum.at[k],
            numh_recv.at[it, k - 1],
            numh_sems.at[it, k],
            (low + side) % 2 * cores + core,
            my,
            (mx + far) % EX,
            mz,
        )
    wide = EX * pixels

    def wait_data(u):
        p, start, _ = UNITS[u]
        first_frame, count = PARTS[p]
        for g in range(first_frame // GROUP, (first_frame + count) // GROUP):
            frames = pl.ds(g * GROUP, GROUP)
            if start == 0:
                own_copy(g).wait()
            for at, n, half in halves(u):
                drain(tile.at[pl.ds(at, n), :, :, frames], data_sems.at[g, 1 + half])

    def unit_w(step, u):
        p, start, count = UNITS[u]
        return w_all[p][step, pl.ds(start, count)].reshape(unit_rows[u], rank)

    def ratios(step_w, step_h, u):
        p, start, count = UNITS[u]
        slots = pl.ds(start, count)
        product = jnp.dot(unit_w(step_w, u), h_all[step_h], preferred_element_type=F32)
        parts = []
        for x in range(EX):
            for k in range(block):
                at = (x * block + k) * LANES
                data = tile[slots, x, k, part_rows(p)].reshape(unit_rows[u], LANES).astype(F32)
                parts.append((data / product[:, at : at + LANES]).astype(BF16))
        return jnp.concatenate(parts, axis=1)

    for it in range(ITERS):
        finish_h(it)
        for u, (p, start, count) in enumerate(UNITS):
            if it == 0:
                wait_w(0, u)
                wait_data(u)
            elif start == 0:
                drain(num_send[p].at[pl.ds(1, SLOTS - 1)], num_sems.at[it - 1, p, 0])
            terms = ratios(it, it, u)
            if u == 0:
                terms = jnp.concatenate([terms, jnp.ones((16, wide), BF16)], axis=0)
            terms = lax.dot_general(
                terms, h_all[it], (((1,), (1,)), ((), ())), preferred_element_type=F32
            )
            num_send[p][pl.ds(start, count)] = terms[: unit_rows[u]].reshape(
                count, PARTS[p][1], rank
            )

            def go(slot, carry):
                to_slot(
                    num_send[p].at[slot],
                    num_recv[p].at[it, slot],
                    num_sems.at[it, p],
                    behind(slot),
                ).start()
                return carry

            lax.fori_loop(max(start, 1), start + count, go, 0)
            if u == 0:
                hsum_all[it, 0] = terms[unit_rows[u] : unit_rows[u] + 1]

                def share(slot, carry):
                    to_slot(
                        hsum_all.at[it, 0], hsum_all.at[it, slot], hsum_sems.at[it], ahead(slot)
                    ).start()
                    return carry

                lax.fori_loop(1, SLOTS, share, 0)

        drain(hsum_all.at[it, pl.ds(1, SLOTS - 1)], hsum_sems.at[it, 1])
        h_sum = hsum_all[it, 0]
        for slot in range(1, SLOTS):
            h_sum = h_sum + hsum_all[it, slot]
        for p in range(2):
            drain(num_recv[p].at[it, pl.ds(1, SLOTS - 1)], num_sems.at[it, p, 1])

            def add(slot, total):
                return total + num_recv[p][it, slot]

            total = lax.fori_loop(1, SLOTS, add, num_send[p][0])
            w_new = w_now[part_rows(p), :] * total / h_sum
            w_now[part_rows(p), :] = w_new
            w_all[p][it + 1, 0] = w_new.astype(BF16)
            send_w(it + 1, p)
        if it == ITERS - 1:
            pltpu.make_async_copy(w_now, w_out, out_sems.at[0]).start()

        if it > 0:
            for far, side in every:
                pair_copy(it - 1, far, side).wait_send()
            for far, side in others:
                chip_copy(it - 1, far, side).wait_send()

        def component_terms(p, far):
            units = [u for u in range(len(UNITS)) if UNITS[u][0] == p]
            count = SLOTS * PARTS[p][1]
            x = (mx + far) % EX
            return lax.dot_general(
                w_all[p][it + 1].reshape(count, rank),
                ratio[
                    pl.ds(unit_start[units[0]], count),
                    pl.ds(pl.multiple_of(x * pixels, pixels), pixels),
                ],
                (((0,), (0,)), ((), ())),
                preferred_element_type=F32,
            ).reshape(n_scan, comps, pixels)

        w_sum = jnp.zeros((1, rank), F32)
        for u in range(len(UNITS)):
            wait_w(it + 1, u)
            ratio[pl.ds(unit_start[u], unit_rows[u]), :] = ratios(it + 1, it, u)
            w_sum = w_sum + jnp.sum(unit_w(it + 1, u).astype(F32), axis=0, keepdims=True)
            if u == 1:
                for far in (1, 0):
                    numh_send[far] = component_terms(0, far)
        wsum_all[it, 0] = w_sum
        for far in (1, 0):
            numh_send[far] = numh_send[far] + component_terms(1, far)
            for side in (1, 0):
                pair_copy(it, far, side).start()
        for j in range(1, mates):
            to_mate(wsum_all.at[it, 0], wsum_all.at[it, j], wsum_sems.at[it], j).start()
        for far in (1, 0):
            for side in (1, 0):
                k = far * 2 + side
                pair_copy(it, far, side).wait_recv()
                here = (low + side) % 2 * cores + core
                pair_sum[k] = numh_send[far, here] + pair_recv[it, k]
                if k > 0:
                    chip_copy(it, far, side).start()
        drain(wsum_all.at[it, pl.ds(1, mates - 1)], wsum_sems.at[it, 1])
        w_sum = wsum_all[it, 0]
        for j in range(1, mates):
            w_sum = w_sum + wsum_all[it, j]
        at = lax.broadcasted_iota(jnp.int32, (comps, rank), 1)
        own = lax.broadcasted_iota(jnp.int32, (comps, rank), 0) + scan * comps
        w_sum = jnp.sum(
            jnp.where(at == own, jnp.broadcast_to(w_sum, (comps, rank)), 0.0),
            axis=1,
            keepdims=True,
        )
        total_h = pair_sum[0]
        for far, side in ((0, 1), (1, 0), (1, 1)):
            chip_copy(it, far, side).wait_recv()
            total_h = total_h + numh_recv[it, far * 2 + side - 1]
        h_new = h_now[...] * total_h / w_sum
        h_now[...] = h_new
        if it == ITERS - 1:
            pltpu.make_async_copy(h_now, h_out, out_sems.at[1]).start()
        else:
            h_all[it + 1, mine[0], mine[1]] = h_new.astype(BF16)
            send_h(it + 1)

    for g in range(groups):
        frames = pl.ds(g * GROUP, GROUP)
        drain(tile.at[pl.ds(1, SLOTS - 1), :, :, frames], data_sems.at[g, 0])
    for step in range(ITERS + 1):
        for p in range(2):
            drain(w_all[p].at[step, pl.ds(1, SLOTS - 1)], w_sems.at[step, p, 0])
    for step in range(ITERS):
        for far, side in others:
            h_chip(step, far, side).wait_send()
        for far, side in every:
            h_pair(step, far, side).wait_send()
        drain(hsum_all.at[step, pl.ds(1, SLOTS - 1)], hsum_sems.at[step, 0])
        drain(wsum_all.at[step, pl.ds(1, mates - 1)], wsum_sems.at[step, 0])
    for p in range(2):
        drain(num_send[p].at[pl.ds(1, SLOTS - 1)], num_sems.at[ITERS - 1, p, 0])
    for far, side in every:
        pair_copy(ITERS - 1, far, side).wait_send()
    for far, side in others:
        chip_copy(ITERS - 1, far, side).wait_send()
    pltpu.make_async_copy(w_now, w_out, out_sems.at[0]).wait()
    pltpu.make_async_copy(h_now, h_out, out_sems.at[1]).wait()


def solution(mesh):
    n_scan = mesh.shape["scan"]
    mates = EX * n_scan

    def local(raw_frames, gain_map, coupling, factor_w, factor_h):
        frames = raw_frames.shape[0]
        rank = factor_w.shape[1]
        comps, pixels = factor_h.shape
        groups = frames // GROUP
        block = pixels // FRAME
        hbm = pl.BlockSpec(memory_space=pl.ANY)
        dma = pltpu.SemaphoreType.DMA
        return pl.pallas_call(
            functools.partial(kernel, n_scan),
            out_shape=(
                jax.ShapeDtypeStruct(factor_w.shape, F32),
                jax.ShapeDtypeStruct(factor_h.shape, F32),
            ),
            in_specs=[hbm] * 5,
            out_specs=(hbm, hbm),
            scratch_shapes=[
                pltpu.VMEM((groups, GROUP * FRAME, LANES), F32),
                pltpu.VMEM((3, FRAME, 8, LANES), F32),
                pltpu.VMEM((FRAME, GROUP, LANES), F32),
                pltpu.VMEM((2, FRAME + 2, GROUP, LANES), F32),
                pltpu.VMEM((EY, EX, EZ, block, frames, LANES), DATA),
                pltpu.VMEM((SLOTS, EX, block, frames, LANES), DATA),
                *[pltpu.VMEM((ITERS + 1, SLOTS, n, rank), BF16) for _, n in PARTS],
                pltpu.VMEM((frames, rank), F32),
                pltpu.VMEM((FRAME, LANES), F32),
                pltpu.VMEM((FRAME, LANES), F32),
                *[pltpu.VMEM((SLOTS, n, rank), F32) for _, n in PARTS],
                *[pltpu.VMEM((ITERS, SLOTS, n, rank), F32) for _, n in PARTS],
                pltpu.VMEM((ITERS, rank, EX * pixels), BF16),
                pltpu.VMEM((comps, pixels), F32),
                pltpu.VMEM((ITERS, SLOTS, 1, rank), F32),
                pltpu.VMEM((SLOTS * frames, EX * pixels), BF16),
                pltpu.VMEM((EX, n_scan, comps, pixels), F32),
                pltpu.VMEM((ITERS, mates // 2, comps, pixels), F32),
                pltpu.VMEM((mates // 2, comps, pixels), F32),
                pltpu.VMEM((ITERS, mates // 2 - 1, comps, pixels), F32),
                pltpu.VMEM((ITERS, mates, 1, rank), F32),
                dma((groups + 4,)),
                dma((groups, 3)),
                dma((groups,)),
                dma((ITERS + 1, 2, 3)),
                dma((ITERS, 2, 2)),
                dma((ITERS, mates // 2, 2)),
                dma((ITERS, mates // 2, 2)),
                dma((ITERS, 2)),
                dma((ITERS, mates // 2, 2)),
                dma((ITERS, mates // 2, 2)),
                dma((ITERS, 2)),
                dma((2,)),
            ],
            compiler_params=pltpu.CompilerParams(
                collective_id=0, has_side_effects=True, vmem_limit_bytes=58 * 1024 * 1024
            ),
        )(raw_frames.reshape(frames * FRAME, LANES), gain_map, coupling, factor_w, factor_h)

    return jax.shard_map(
        local,
        mesh=mesh,
        in_specs=(
            P(("scan", "pix"), None, None),
            P(),
            P(),
            P(("scan", "pix"), None),
            P("scan", "pix"),
        ),
        out_specs=(P(("scan", "pix"), None), P("scan", "pix")),
        check_vma=False,
    )
```

```python
import functools

import jax
import jax.numpy as jnp
from jax import lax
from jax.experimental import pallas as pl
from jax.experimental.pallas import tpu as pltpu
from jax.sharding import PartitionSpec as P

SWEEPS = 4
ITERS = 2
FRAME = 128
LANES = 128
EY, EX, EZ = 4, 2, 4
SLOTS = EY * EZ
GROUP = 16
ROWS = 64
DATA = jnp.bfloat16
PARTS = tuple((g * GROUP, GROUP) for g in range(3))
UNITS = tuple((g, 0, SLOTS) for g in range(3))
HALF = SLOTS // 2

MESH = pl.DeviceIdType.MESH
F32 = jnp.float32
BF16 = jnp.bfloat16


def kernel(
    n_scan,
    raw_ref,
    gain_ref,
    couple_ref,
    w_ref,
    h_ref,
    w_out,
    h_out,
    raw_v,
    maps,
    scaled,
    field,
    stretch,
    charge,
    tile,
    w_all,
    w_now,
    gain_v,
    couple_v,
    num_send,
    num_recv,
    h_all,
    h_now,
    hsum_all,
    ratio,
    numh_send,
    pair_recv,
    pair_sum,
    numh_recv,
    wsum_all,
    raw_sem,
    data_sems,
    own_sem,
    w_sems,
    num_sems,
    h_sems,
    h_pair_sems,
    hsum_sems,
    pair_sems,
    numh_sems,
    wsum_sems,
):
    rows, rank = w_ref.shape
    comps, pixels = h_ref.shape
    block = pixels // FRAME
    groups = rows // GROUP
    mates = EX * n_scan
    scan = lax.axis_index("scan")
    pix = lax.axis_index("pix")
    my, mx, mz = pix // (EX * EZ), (pix // EZ) % EX, pix % EZ
    cores = n_scan // 2
    low, core = scan // cores, scan % cores
    twin = (core + 1) % cores

    def ahead(slot):
        return (my + slot // EZ) % EY, (mz + slot % EZ) % EZ

    def behind(slot):
        return (my + EY - slot // EZ) % EY, (mz + EZ - slot % EZ) % EZ

    def mate(j):
        other = (mx * n_scan + scan + j) % mates
        return other % n_scan, other // n_scan

    def remote(src, dst, sems, to_scan, y, x, z, part=0):
        return pltpu.make_async_remote_copy(
            src_ref=src,
            dst_ref=dst,
            send_sem=sems.at[0],
            recv_sem=sems.at[1 + part],
            device_id=(to_scan, (y * EX + x) * EZ + z),
            device_id_type=MESH,
        )

    def to_slot(src, dst, sems, where, part=0):
        y, z = where
        return remote(src, dst, sems, scan, y, mx, z, part)

    def to_mate(src, dst, sems, j):
        to_scan, x = mate(j)
        return remote(src, dst, sems, to_scan, my, x, mz)

    def drain(ref, sem):
        pltpu.make_async_copy(ref, ref, sem).wait()

    def fetch(g):
        return pltpu.make_async_copy(
            raw_ref.at[pl.ds(g * GROUP * FRAME, GROUP * FRAME)], raw_v.at[g], raw_sem.at[g]
        )

    small = [
        pltpu.make_async_copy(src, dst, raw_sem.at[groups + i])
        for i, (src, dst) in enumerate(
            ((w_ref, w_now), (h_ref, h_now), (gain_ref, gain_v), (couple_ref, couple_v))
        )
    ]
    for copy in small:
        copy.start()
    for g in range(groups):
        fetch(g).start()

    barrier = pltpu.get_barrier_semaphore()

    def greet(slot, carry):
        y, z = ahead(slot)
        pl.semaphore_signal(
            barrier, inc=1, device_id=(scan, (y * EX + mx) * EZ + z), device_id_type=MESH
        )
        return carry

    lax.fori_loop(1, SLOTS, greet, 0)
    for j in range(1, mates):
        to_scan, x = mate(j)
        pl.semaphore_signal(
            barrier, inc=1, device_id=(to_scan, (my * EX + x) * EZ + mz), device_id_type=MESH
        )

    for copy in small:
        copy.wait()

    def part_rows(p):
        return pl.ds(*PARTS[p])

    def send_w(step, p):
        for copy_slots in ((1, HALF), (HALF, SLOTS)):

            def go(slot, carry):
                to_slot(
                    w_all[p].at[step, 0],
                    w_all[p].at[step, slot],
                    w_sems.at[step, p],
                    ahead(slot),
                    copy_slots[0] // HALF,
                ).start()
                return carry

            lax.fori_loop(*copy_slots, go, 0)

    def halves(u):
        _, start, count = UNITS[u]
        both = ((1, HALF - 1, 0), (HALF, HALF, 1))
        return [h for h in both if start <= h[0] < start + count]

    def wait_w(step, u):
        p = UNITS[u][0]
        for start, count, half in halves(u):
            drain(w_all[p].at[step, pl.ds(start, count)], w_sems.at[step, p, 1 + half])

    def place(far, side, of_core):
        at = (low + side) % 2 * cores + of_core
        return (
            pl.ds(pl.multiple_of(at * comps, comps), comps),
            pl.ds(pl.multiple_of((mx + far) % EX * pixels, pixels), pixels),
        )

    mine = place(0, 0, core)

    def h_chip(step, far, side):
        own = h_all.at[step, mine[0], mine[1]]
        return remote(
            own,
            own,
            h_sems.at[step, far * 2 + side],
            (low + side) % 2 * cores + core,
            my,
            (mx + far) % EX,
            mz,
        )

    def h_pair(step, far, side):
        at = place(far, side, core)
        part = h_all.at[step, at[0], at[1]]
        return remote(
            part, part, h_pair_sems.at[step, far * 2 + side], low * cores + twin, my, mx, mz
        )

    others = ((1, 0), (1, 1), (0, 1))
    every = ((0, 0),) + others

    def send_h(step):
        for far, side in others:
            h_chip(step, far, side).start()
        h_pair(step, 0, 0).start()

    def finish_h(step):
        for far, side in others[::-1]:
            h_chip(step, far, side).wait_recv()
            h_pair(step, far, side).start()
        for far, side in every:
            h_pair(step, far, side).wait_recv()

    for p in range(len(PARTS)):
        w_all[p][0, 0] = w_now[part_rows(p), :].astype(BF16)
    h_all[0, mine[0], mine[1]] = h_now[...].astype(BF16)

    def meet():
        pl.semaphore_wait(barrier, SLOTS - 1 + mates - 1)
        send_h(0)
        for p in range(len(PARTS)):
            send_w(0, p)

    coupling = couple_v[...]
    inverse = 1.0 / (1.0 + 4.0 * coupling)
    gain = gain_v[...]
    for i, value in enumerate((gain, gain * inverse, coupling * inverse)):
        maps[i] = jnp.broadcast_to(value[:, None, :], (FRAME, 8, LANES))

    shape = (block, rows, LANES)
    turn = [lax.broadcasted_iota(jnp.int32, shape, i) for i in range(3)]
    turn = jnp.bitwise_and(107 * turn[0] + 193 * turn[1] + 145 * turn[2], 255)
    factor = 1.0 + (turn.astype(F32) - 127.5) * (2.0**-12)
    stretch[0] = factor
    stretch[1] = 1.0 / factor

    lane = lax.broadcasted_iota(jnp.int32, (ROWS, GROUP, LANES), 2)
    first, last = lane == 0, lane == LANES - 1

    for i in range(2):
        edge = jnp.zeros((GROUP, LANES), F32)
        field[i, 0] = edge
        field[i, FRAME + 1] = edge

    def correct(g, between=None):
        def map_rows(i, at):
            value = maps[i, pl.ds(at, ROWS)]
            return jnp.concatenate([value] * (GROUP // 8), axis=1)

        def start(c, carry):
            at = c * 8
            for i in range(8):
                raw = raw_v[g, pl.ds(at + i, GROUP, stride=FRAME), :]
                tall = [maps[m, at + i] for m in range(2)]
                gain_row, scaled_row = [
                    jnp.concatenate([v] * (GROUP // 8), axis=0) for v in tall
                ]
                field[0, at + i + 1] = raw * gain_row
                scaled[at + i] = raw * scaled_row
            return carry

        lax.fori_loop(0, FRAME // 8, start, 0)
        for s in range(SWEEPS):

            def sweep(c, carry):
                at = c * ROWS
                rows_in = field[s % 2, pl.ds(at, ROWS + 2)]
                mid = rows_in[1:-1]
                left = jnp.where(first, 0.0, pltpu.roll(mid, 1, 2))
                right = jnp.where(last, 0.0, pltpu.roll(mid, LANES - 1, 2))
                value = scaled[pl.ds(at, ROWS)] + map_rows(2, at) * (
                    (rows_in[:-2] + rows_in[2:]) + (left + right)
                )
                if s == SWEEPS - 1:
                    slabs = ROWS // (EX * EZ * block)
                    frames = pl.ds(g * GROUP, GROUP)
                    value = value.reshape(slabs * EX * EZ, block, GROUP, LANES)
                    value = (value * stretch[0, :, frames][None]).astype(charge.dtype)
                    charge[pl.ds(c * slabs, slabs), :, :, :, frames, :] = value.reshape(
                        slabs, EX, EZ, block, GROUP, LANES
                    )
                else:
                    field[(s + 1) % 2, pl.ds(at + 1, ROWS)] = value
                return carry

            lax.fori_loop(0, FRAME // ROWS, sweep, 0)
            if s == 1 and between is not None:
                between()

    def own_copy(g):
        frames = pl.ds(g * GROUP, GROUP)
        return pltpu.make_async_copy(
            charge.at[my, :, mz, :, frames], tile.at[0, :, :, frames], own_sem.at[g]
        )

    for g in range(groups):
        fetch(g).wait()
        correct(g, meet if g == 0 else None)
        own_copy(g).start()
        frames = pl.ds(g * GROUP, GROUP)

        for half, (start, stop) in enumerate(((1, HALF), (HALF, SLOTS))):

            def go(slot, carry):
                y, z = ahead(slot)
                to_slot(
                    charge.at[y, :, z, :, frames],
                    tile.at[slot, :, :, frames],
                    data_sems.at[g],
                    (y, z),
                    half,
                ).start()
                return carry

            lax.fori_loop(start, stop, go, 0)

    wide = EX * pixels
    unit_rows = [count * PARTS[p][1] for p, _, count in UNITS]
    unit_start = [sum(unit_rows[:u]) for u in range(len(UNITS))]

    def pair_copy(it, far, side):
        k = far * 2 + side
        there = (low + side) % 2 * cores + twin
        return remote(
            numh_send.at[far, there],
            pair_recv.at[it, k],
            pair_sems.at[it, k],
            low * cores + twin,
            my,
            mx,
            mz,
        )

    def chip_copy(it, far, side):
        k = far * 2 + side
        return remote(
            pair_sum.at[k],
            numh_recv.at[it, k - 1],
            numh_sems.at[it, k],
            (low + side) % 2 * cores + core,
            my,
            (mx + far) % EX,
            mz,
        )
    wide = EX * pixels

    def wait_data(u):
        p, start, _ = UNITS[u]
        first_frame, count = PARTS[p]
        for g in range(first_frame // GROUP, (first_frame + count) // GROUP):
            frames = pl.ds(g * GROUP, GROUP)
            if start == 0:
                own_copy(g).wait()
            for at, n, half in halves(u):
                drain(tile.at[pl.ds(at, n), :, :, frames], data_sems.at[g, 1 + half])

    def unit_w(step, u):
        p, start, count = UNITS[u]
        return w_all[p][step, pl.ds(start, count)].reshape(unit_rows[u], rank)

    def ratios(step_w, step_h, u):
        p, start, count = UNITS[u]
        slots = pl.ds(start, count)
        product = jnp.dot(unit_w(step_w, u), h_all[step_h], preferred_element_type=F32)
        parts = []
        for x in range(EX):
            for k in range(block):
                at = (x * block + k) * LANES
                data = tile[slots, x, k, part_rows(p)].astype(F32) * stretch[1, k, part_rows(p)][None]
                data = data.reshape(unit_rows[u], LANES)
                parts.append((data / product[:, at : at + LANES]).astype(BF16))
        return jnp.concatenate(parts, axis=1)

    for it in range(ITERS):
        finish_h(it)
        for u, (p, start, count) in enumerate(UNITS):
            if it == 0:
                wait_w(0, u)
                wait_data(u)
            elif start == 0:
                drain(num_send[p].at[pl.ds(1, SLOTS - 1)], num_sems.at[it - 1, p, 0])
            terms = ratios(it, it, u)
            if u == 0:
                terms = jnp.concatenate([terms, jnp.ones((16, wide), BF16)], axis=0)
            terms = lax.dot_general(
                terms, h_all[it], (((1,), (1,)), ((), ())), preferred_element_type=F32
            )
            num_send[p][pl.ds(start, count)] = terms[: unit_rows[u]].reshape(
                count, PARTS[p][1], rank
            )

            def go(slot, carry):
                to_slot(
                    num_send[p].at[slot],
                    num_recv[p].at[it, slot],
                    num_sems.at[it, p],
                    behind(slot),
                ).start()
                return carry

            lax.fori_loop(max(start, 1), start + count, go, 0)
            if u == 0:
                hsum_all[it, 0] = terms[unit_rows[u] : unit_rows[u] + 1]

                def share(slot, carry):
                    to_slot(
                        hsum_all.at[it, 0], hsum_all.at[it, slot], hsum_sems.at[it], ahead(slot)
                    ).start()
                    return carry

                lax.fori_loop(1, SLOTS, share, 0)

        drain(hsum_all.at[it, pl.ds(1, SLOTS - 1)], hsum_sems.at[it, 1])
        h_sum = hsum_all[it, 0]
        for slot in range(1, SLOTS):
            h_sum = h_sum + hsum_all[it, slot]
        for p in range(len(PARTS)):
            drain(num_recv[p].at[it, pl.ds(1, SLOTS - 1)], num_sems.at[it, p, 1])

            def add(slot, total):
                return total + num_recv[p][it, slot]

            total = lax.fori_loop(1, SLOTS, add, num_send[p][0])
            w_new = w_now[part_rows(p), :] * total / h_sum
            w_now[part_rows(p), :] = w_new
            w_all[p][it + 1, 0] = w_new.astype(BF16)
            send_w(it + 1, p)
        if it == ITERS - 1:
            w_out[...] = w_now[...]

        if it > 0:
            for far, side in every:
                pair_copy(it - 1, far, side).wait_send()
            for far, side in others:
                chip_copy(it - 1, far, side).wait_send()

        def component_terms(p, far):
            units = [u for u in range(len(UNITS)) if UNITS[u][0] == p]
            count = SLOTS * PARTS[p][1]
            x = (mx + far) % EX
            return lax.dot_general(
                w_all[p][it + 1].reshape(count, rank),
                ratio[
                    pl.ds(unit_start[units[0]], count),
                    pl.ds(pl.multiple_of(x * pixels, pixels), pixels),
                ],
                (((0,), (0,)), ((), ())),
                preferred_element_type=F32,
            ).reshape(n_scan, comps, pixels)

        w_sum = jnp.zeros((1, rank), F32)
        for u in range(len(UNITS)):
            wait_w(it + 1, u)
            ratio[pl.ds(unit_start[u], unit_rows[u]), :] = ratios(it + 1, it, u)
            w_sum = w_sum + jnp.sum(unit_w(it + 1, u).astype(F32), axis=0, keepdims=True)
            p = UNITS[u][0]
            if p < len(PARTS) - 1 and UNITS[u + 1][0] > p:
                for far in (1, 0):
                    terms = component_terms(p, far)
                    numh_send[far] = terms if p == 0 else numh_send[far] + terms
        wsum_all[it, 0] = w_sum
        for far in (1, 0):
            numh_send[far] = numh_send[far] + component_terms(len(PARTS) - 1, far)
            for side in (1, 0):
                pair_copy(it, far, side).start()
        for j in range(1, mates):
            to_mate(wsum_all.at[it, 0], wsum_all.at[it, j], wsum_sems.at[it], j).start()
        for far in (1, 0):
            for side in (1, 0):
                k = far * 2 + side
                pair_copy(it, far, side).wait_recv()
                here = (low + side) % 2 * cores + core
                pair_sum[k] = numh_send[far, here] + pair_recv[it, k]
                if k > 0:
                    chip_copy(it, far, side).start()
        drain(wsum_all.at[it, pl.ds(1, mates - 1)], wsum_sems.at[it, 1])
        w_sum = wsum_all[it, 0]
        for j in range(1, mates):
            w_sum = w_sum + wsum_all[it, j]
        at = lax.broadcasted_iota(jnp.int32, (comps, rank), 1)
        own = lax.broadcasted_iota(jnp.int32, (comps, rank), 0) + scan * comps
        w_sum = jnp.sum(
            jnp.where(at == own, jnp.broadcast_to(w_sum, (comps, rank)), 0.0),
            axis=1,
            keepdims=True,
        )
        total_h = pair_sum[0]
        for far, side in ((0, 1), (1, 0), (1, 1)):
            chip_copy(it, far, side).wait_recv()
            total_h = total_h + numh_recv[it, far * 2 + side - 1]
        h_new = h_now[...] * total_h / w_sum
        if it == ITERS - 1:
            h_out[...] = h_new
        else:
            h_now[...] = h_new
            h_all[it + 1, mine[0], mine[1]] = h_new.astype(BF16)
            send_h(it + 1)

    for g in range(groups):
        frames = pl.ds(g * GROUP, GROUP)
        drain(tile.at[pl.ds(1, SLOTS - 1), :, :, frames], data_sems.at[g, 0])
    for step in range(ITERS + 1):
        for p in range(len(PARTS)):
            drain(w_all[p].at[step, pl.ds(1, SLOTS - 1)], w_sems.at[step, p, 0])
    for step in range(ITERS):
        for far, side in others:
            h_chip(step, far, side).wait_send()
        for far, side in every:
            h_pair(step, far, side).wait_send()
        drain(hsum_all.at[step, pl.ds(1, SLOTS - 1)], hsum_sems.at[step, 0])
        drain(wsum_all.at[step, pl.ds(1, mates - 1)], wsum_sems.at[step, 0])
    for p in range(len(PARTS)):
        drain(num_send[p].at[pl.ds(1, SLOTS - 1)], num_sems.at[ITERS - 1, p, 0])
    for far, side in every:
        pair_copy(ITERS - 1, far, side).wait_send()
    for far, side in others:
        chip_copy(ITERS - 1, far, side).wait_send()


def solution(mesh):
    n_scan = mesh.shape["scan"]
    mates = EX * n_scan

    def local(raw_frames, gain_map, coupling, factor_w, factor_h):
        frames = raw_frames.shape[0]
        rank = factor_w.shape[1]
        comps, pixels = factor_h.shape
        groups = frames // GROUP
        block = pixels // FRAME
        hbm = pl.BlockSpec(memory_space=pl.ANY)
        vmem = pl.BlockSpec(memory_space=pltpu.VMEM)
        dma = pltpu.SemaphoreType.DMA
        return pl.pallas_call(
            functools.partial(kernel, n_scan),
            out_shape=(
                pltpu.VMEM(factor_w.shape, F32),
                pltpu.VMEM(factor_h.shape, F32),
            ),
            in_specs=[hbm] * 5,
            out_specs=(vmem, vmem),
            scratch_shapes=[
                pltpu.VMEM((groups, GROUP * FRAME, LANES), F32),
                pltpu.VMEM((3, FRAME, 8, LANES), F32),
                pltpu.VMEM((FRAME, GROUP, LANES), F32),
                pltpu.VMEM((2, FRAME + 2, GROUP, LANES), F32),
                pltpu.VMEM((2, block, frames, LANES), F32),
                pltpu.VMEM((EY, EX, EZ, block, frames, LANES), DATA),
                pltpu.VMEM((SLOTS, EX, block, frames, LANES), DATA),
                tuple(pltpu.VMEM((ITERS + 1, SLOTS, n, rank), BF16) for _, n in PARTS),
                pltpu.VMEM((frames, rank), F32),
                pltpu.VMEM((FRAME, LANES), F32),
                pltpu.VMEM((FRAME, LANES), F32),
                tuple(pltpu.VMEM((SLOTS, n, rank), F32) for _, n in PARTS),
                tuple(pltpu.VMEM((ITERS, SLOTS, n, rank), F32) for _, n in PARTS),
                pltpu.VMEM((ITERS, rank, EX * pixels), BF16),
                pltpu.VMEM((comps, pixels), F32),
                pltpu.VMEM((ITERS, SLOTS, 1, rank), F32),
                pltpu.VMEM((SLOTS * frames, EX * pixels), BF16),
                pltpu.VMEM((EX, n_scan, comps, pixels), F32),
                pltpu.VMEM((ITERS, mates // 2, comps, pixels), F32),
                pltpu.VMEM((mates // 2, comps, pixels), F32),
                pltpu.VMEM((ITERS, mates // 2 - 1, comps, pixels), F32),
                pltpu.VMEM((ITERS, mates, 1, rank), F32),
                dma((groups + 4,)),
                dma((groups, 3)),
                dma((groups,)),
                dma((ITERS + 1, len(PARTS), 3)),
                dma((ITERS, len(PARTS), 2)),
                dma((ITERS, mates // 2, 2)),
                dma((ITERS, mates // 2, 2)),
                dma((ITERS, 2)),
                dma((ITERS, mates // 2, 2)),
                dma((ITERS, mates // 2, 2)),
                dma((ITERS, 2)),
            ],
            compiler_params=pltpu.CompilerParams(
                collective_id=0, has_side_effects=True, vmem_limit_bytes=58 * 1024 * 1024
            ),
        )(raw_frames.reshape(frames * FRAME, LANES), gain_map, coupling, factor_w, factor_h)

    return jax.shard_map(
        local,
        mesh=mesh,
        in_specs=(
            P(("scan", "pix"), None, None),
            P(),
            P(),
            P(("scan", "pix"), None),
            P("scan", "pix"),
        ),
        out_specs=(P(("scan", "pix"), None), P("scan", "pix")),
        check_vma=False,
    )
```

```python
import functools

import jax
import jax.numpy as jnp
from jax import lax
from jax.experimental import pallas as pl
from jax.experimental.pallas import tpu as pltpu
from jax.sharding import PartitionSpec as P

SWEEPS = 4
ITERS = 2
FRAME = 128
LANES = 128
EY, EX, EZ = 4, 2, 4
SLOTS = EY * EZ
GROUP = 16
ROWS = 64
DATA = jnp.bfloat16
PARTS = tuple((g * GROUP, GROUP) for g in range(3))
UNITS = tuple((g, 0, SLOTS) for g in range(3))
HALF = SLOTS // 2

MESH = pl.DeviceIdType.MESH
F32 = jnp.float32
BF16 = jnp.bfloat16


def kernel(
    n_scan,
    raw_ref,
    gain_ref,
    couple_ref,
    w_ref,
    h_ref,
    w_out,
    h_out,
    raw_v,
    maps,
    scaled,
    field,
    stretch,
    charge,
    tile,
    w_all,
    w_now,
    gain_v,
    couple_v,
    num_send,
    num_recv,
    h_all,
    h_now,
    hsum_all,
    ratio,
    numh_send,
    pair_recv,
    pair_sum,
    numh_recv,
    wsum_all,
    raw_sem,
    data_sems,
    own_sem,
    w_sems,
    num_sems,
    h_sems,
    h_pair_sems,
    hsum_sems,
    pair_sems,
    numh_sems,
    wsum_sems,
):
    rows, rank = w_ref.shape
    comps, pixels = h_ref.shape
    block = pixels // FRAME
    groups = rows // GROUP
    mates = EX * n_scan
    scan = lax.axis_index("scan")
    pix = lax.axis_index("pix")
    my, mx, mz = pix // (EX * EZ), (pix // EZ) % EX, pix % EZ
    cores = n_scan // 2
    low, core = scan // cores, scan % cores
    twin = (core + 1) % cores

    def ahead(slot):
        return (my + slot // EZ) % EY, (mz + slot % EZ) % EZ

    def behind(slot):
        return (my + EY - slot // EZ) % EY, (mz + EZ - slot % EZ) % EZ

    def mate(j):
        other = (mx * n_scan + scan + j) % mates
        return other % n_scan, other // n_scan

    def in_order(go):
        for slot in sorted(range(1, SLOTS), key=lambda d: (min(d // EZ, EY - d // EZ) + min(d % EZ, EZ - d % EZ)), reverse=True):
            go(slot)

    def remote(src, dst, sems, to_scan, y, x, z, part=0):
        return pltpu.make_async_remote_copy(
            src_ref=src,
            dst_ref=dst,
            send_sem=sems.at[0],
            recv_sem=sems.at[1 + part],
            device_id=(to_scan, (y * EX + x) * EZ + z),
            device_id_type=MESH,
        )

    def to_slot(src, dst, sems, where, part=0):
        y, z = where
        return remote(src, dst, sems, scan, y, mx, z, part)

    def to_mate(src, dst, sems, j):
        to_scan, x = mate(j)
        return remote(src, dst, sems, to_scan, my, x, mz)

    def drain(ref, sem):
        pltpu.make_async_copy(ref, ref, sem).wait()

    def fetch(g):
        return pltpu.make_async_copy(
            raw_ref.at[pl.ds(g * GROUP * FRAME, GROUP * FRAME)], raw_v.at[g], raw_sem.at[g]
        )

    small = [
        pltpu.make_async_copy(src, dst, raw_sem.at[groups + i])
        for i, (src, dst) in enumerate(
            ((w_ref, w_now), (h_ref, h_now), (gain_ref, gain_v), (couple_ref, couple_v))
        )
    ]
    for copy in small:
        copy.start()
    for g in range(groups):
        fetch(g).start()

    barrier = pltpu.get_barrier_semaphore()

    def greet(slot, carry):
        y, z = ahead(slot)
        pl.semaphore_signal(
            barrier, inc=1, device_id=(scan, (y * EX + mx) * EZ + z), device_id_type=MESH
        )
        return carry

    lax.fori_loop(1, SLOTS, greet, 0)
    for j in range(1, mates):
        to_scan, x = mate(j)
        pl.semaphore_signal(
            barrier, inc=1, device_id=(to_scan, (my * EX + x) * EZ + mz), device_id_type=MESH
        )

    for copy in small:
        copy.wait()

    def part_rows(p):
        return pl.ds(*PARTS[p])

    def send_w(step, p):
        def go(slot):
            to_slot(
                w_all[p].at[step, 0],
                w_all[p].at[step, slot],
                w_sems.at[step, p],
                ahead(slot),
                slot // HALF,
            ).start()

        in_order(go)

    def halves(u):
        _, start, count = UNITS[u]
        both = ((1, HALF - 1, 0), (HALF, HALF, 1))
        return [h for h in both if start <= h[0] < start + count]

    def wait_w(step, u):
        p = UNITS[u][0]
        for start, count, half in halves(u):
            drain(w_all[p].at[step, pl.ds(start, count)], w_sems.at[step, p, 1 + half])

    def place(far, side, of_core):
        at = (low + side) % 2 * cores + of_core
        return (
            pl.ds(pl.multiple_of(at * comps, comps), comps),
            pl.ds(pl.multiple_of((mx + far) % EX * pixels, pixels), pixels),
        )

    mine = place(0, 0, core)

    def h_chip(step, far, side):
        own = h_all.at[step, mine[0], mine[1]]
        return remote(
            own,
            own,
            h_sems.at[step, far * 2 + side],
            (low + side) % 2 * cores + core,
            my,
            (mx + far) % EX,
            mz,
        )

    def h_pair(step, far, side):
        at = place(far, side, core)
        part = h_all.at[step, at[0], at[1]]
        return remote(
            part, part, h_pair_sems.at[step, far * 2 + side], low * cores + twin, my, mx, mz
        )

    others = ((1, 0), (1, 1), (0, 1))
    every = ((0, 0),) + others

    def send_h(step):
        for far, side in others:
            h_chip(step, far, side).start()
        h_pair(step, 0, 0).start()

    def finish_h(step):
        for far, side in others[::-1]:
            h_chip(step, far, side).wait_recv()
            h_pair(step, far, side).start()
        for far, side in every:
            h_pair(step, far, side).wait_recv()

    for p in range(len(PARTS)):
        w_all[p][0, 0] = w_now[part_rows(p), :].astype(BF16)
    h_all[0, mine[0], mine[1]] = h_now[...].astype(BF16)

    def meet():
        pl.semaphore_wait(barrier, SLOTS - 1 + mates - 1)
        send_h(0)
        for p in range(len(PARTS)):
            send_w(0, p)

    coupling = couple_v[...]
    inverse = 1.0 / (1.0 + 4.0 * coupling)
    gain = gain_v[...]
    for i, value in enumerate((gain, gain * inverse, coupling * inverse)):
        maps[i] = jnp.broadcast_to(value[:, None, :], (FRAME, 8, LANES))

    shape = (block, rows, LANES)
    turn = [lax.broadcasted_iota(jnp.int32, shape, i) for i in range(3)]
    turn = jnp.bitwise_and(107 * turn[0] + 193 * turn[1] + 145 * turn[2], 255)
    factor = 1.0 + (turn.astype(F32) - 127.5) * (2.0**-12)
    stretch[0] = factor
    stretch[1] = 1.0 / factor

    lane = lax.broadcasted_iota(jnp.int32, (ROWS, GROUP, LANES), 2)
    first, last = lane == 0, lane == LANES - 1

    for i in range(2):
        edge = jnp.zeros((GROUP, LANES), F32)
        field[i, 0] = edge
        field[i, FRAME + 1] = edge

    def correct(g, between=None):
        def map_rows(i, at):
            value = maps[i, pl.ds(at, ROWS)]
            return jnp.concatenate([value] * (GROUP // 8), axis=1)

        def start(c, carry):
            at = c * 8
            for i in range(8):
                raw = raw_v[g, pl.ds(at + i, GROUP, stride=FRAME), :]
                tall = [maps[m, at + i] for m in range(2)]
                gain_row, scaled_row = [
                    jnp.concatenate([v] * (GROUP // 8), axis=0) for v in tall
                ]
                field[0, at + i + 1] = raw * gain_row
                scaled[at + i] = raw * scaled_row
            return carry

        lax.fori_loop(0, FRAME // 8, start, 0)
        for s in range(SWEEPS):

            def sweep(c, carry):
                at = c * ROWS
                rows_in = field[s % 2, pl.ds(at, ROWS + 2)]
                mid = rows_in[1:-1]
                left = jnp.where(first, 0.0, pltpu.roll(mid, 1, 2))
                right = jnp.where(last, 0.0, pltpu.roll(mid, LANES - 1, 2))
                value = scaled[pl.ds(at, ROWS)] + map_rows(2, at) * (
                    (rows_in[:-2] + rows_in[2:]) + (left + right)
                )
                if s == SWEEPS - 1:
                    slabs = ROWS // (EX * EZ * block)
                    frames = pl.ds(g * GROUP, GROUP)
                    value = value.reshape(slabs * EX * EZ, block, GROUP, LANES)
                    value = (value * stretch[0, :, frames][None]).astype(charge.dtype)
                    charge[pl.ds(c * slabs, slabs), :, :, :, frames, :] = value.reshape(
                        slabs, EX, EZ, block, GROUP, LANES
                    )
                else:
                    field[(s + 1) % 2, pl.ds(at + 1, ROWS)] = value
                return carry

            lax.fori_loop(0, FRAME // ROWS, sweep, 0)
            if s == 0 and between is not None:
                between()

    def own_copy(g):
        frames = pl.ds(g * GROUP, GROUP)
        return pltpu.make_async_copy(
            charge.at[my, :, mz, :, frames], tile.at[0, :, :, frames], own_sem.at[g]
        )

    for g in range(groups):
        fetch(g).wait()
        correct(g, meet if g == 0 else None)
        own_copy(g).start()
        frames = pl.ds(g * GROUP, GROUP)

        def go(slot):
            y, z = ahead(slot)
            to_slot(
                charge.at[y, :, z, :, frames],
                tile.at[slot, :, :, frames],
                data_sems.at[g],
                (y, z),
                slot // HALF,
            ).start()

        in_order(go)

    wide = EX * pixels
    unit_rows = [count * PARTS[p][1] for p, _, count in UNITS]
    unit_start = [sum(unit_rows[:u]) for u in range(len(UNITS))]

    def pair_copy(it, far, side):
        k = far * 2 + side
        there = (low + side) % 2 * cores + twin
        return remote(
            numh_send.at[far, there],
            pair_recv.at[it, k],
            pair_sems.at[it, k],
            low * cores + twin,
            my,
            mx,
            mz,
        )

    def chip_copy(it, far, side):
        k = far * 2 + side
        return remote(
            pair_sum.at[k],
            numh_recv.at[it, k - 1],
            numh_sems.at[it, k],
            (low + side) % 2 * cores + core,
            my,
            (mx + far) % EX,
            mz,
        )
    wide = EX * pixels

    def wait_data(u):
        p, start, _ = UNITS[u]
        first_frame, count = PARTS[p]
        for g in range(first_frame // GROUP, (first_frame + count) // GROUP):
            frames = pl.ds(g * GROUP, GROUP)
            if start == 0:
                own_copy(g).wait()
            for at, n, half in halves(u):
                drain(tile.at[pl.ds(at, n), :, :, frames], data_sems.at[g, 1 + half])

    def unit_w(step, u):
        p, start, count = UNITS[u]
        return w_all[p][step, pl.ds(start, count)].reshape(unit_rows[u], rank)

    def ratios(step_w, step_h, u):
        p, start, count = UNITS[u]
        slots = pl.ds(start, count)
        product = jnp.dot(unit_w(step_w, u), h_all[step_h], preferred_element_type=F32)
        parts = []
        for x in range(EX):
            for k in range(block):
                at = (x * block + k) * LANES
                data = tile[slots, x, k, part_rows(p)].astype(F32) * stretch[1, k, part_rows(p)][None]
                data = data.reshape(unit_rows[u], LANES)
                parts.append((data / product[:, at : at + LANES]).astype(BF16))
        return jnp.concatenate(parts, axis=1)

    for it in range(ITERS):
        finish_h(it)
        for u, (p, start, count) in enumerate(UNITS):
            if it == 0:
                wait_w(0, u)
                wait_data(u)
            elif start == 0:
                drain(num_send[p].at[pl.ds(1, SLOTS - 1)], num_sems.at[it - 1, p, 0])
            terms = ratios(it, it, u)
            if u == 0:
                terms = jnp.concatenate([terms, jnp.ones((16, wide), BF16)], axis=0)
            terms = lax.dot_general(
                terms, h_all[it], (((1,), (1,)), ((), ())), preferred_element_type=F32
            )
            num_send[p][pl.ds(start, count)] = terms[: unit_rows[u]].reshape(
                count, PARTS[p][1], rank
            )

            def go(slot):
                to_slot(
                    num_send[p].at[slot],
                    num_recv[p].at[it, slot],
                    num_sems.at[it, p],
                    behind(slot),
                ).start()

            in_order(go)
            if u == 0:
                hsum_all[it, 0] = terms[unit_rows[u] : unit_rows[u] + 1]

                def share(slot, carry):
                    to_slot(
                        hsum_all.at[it, 0], hsum_all.at[it, slot], hsum_sems.at[it], ahead(slot)
                    ).start()
                    return carry

                lax.fori_loop(1, SLOTS, share, 0)

        drain(hsum_all.at[it, pl.ds(1, SLOTS - 1)], hsum_sems.at[it, 1])
        h_sum = hsum_all[it, 0]
        for slot in range(1, SLOTS):
            h_sum = h_sum + hsum_all[it, slot]
        for p in range(len(PARTS)):
            drain(num_recv[p].at[it, pl.ds(1, SLOTS - 1)], num_sems.at[it, p, 1])

            def add(slot, total):
                return total + num_recv[p][it, slot]

            total = lax.fori_loop(1, SLOTS, add, num_send[p][0])
            w_new = w_now[part_rows(p), :] * total / h_sum
            w_now[part_rows(p), :] = w_new
            w_all[p][it + 1, 0] = w_new.astype(BF16)
            send_w(it + 1, p)
        if it == ITERS - 1:
            w_out[...] = w_now[...]

        if it > 0:
            for far, side in every:
                pair_copy(it - 1, far, side).wait_send()
            for far, side in others:
                chip_copy(it - 1, far, side).wait_send()

        def component_terms(p, far):
            units = [u for u in range(len(UNITS)) if UNITS[u][0] == p]
            count = SLOTS * PARTS[p][1]
            x = (mx + far) % EX
            return lax.dot_general(
                w_all[p][it + 1].reshape(count, rank),
                ratio[
                    pl.ds(unit_start[units[0]], count),
                    pl.ds(pl.multiple_of(x * pixels, pixels), pixels),
                ],
                (((0,), (0,)), ((), ())),
                preferred_element_type=F32,
            ).reshape(n_scan, comps, pixels)

        w_sum = jnp.zeros((1, rank), F32)
        for u in range(len(UNITS)):
            wait_w(it + 1, u)
            ratio[pl.ds(unit_start[u], unit_rows[u]), :] = ratios(it + 1, it, u)
            w_sum = w_sum + jnp.sum(unit_w(it + 1, u).astype(F32), axis=0, keepdims=True)
            p = UNITS[u][0]
            if p < len(PARTS) - 1 and UNITS[u + 1][0] > p:
                for far in (1, 0):
                    terms = component_terms(p, far)
                    numh_send[far] = terms if p == 0 else numh_send[far] + terms
        wsum_all[it, 0] = w_sum
        for far in (1, 0):
            numh_send[far] = numh_send[far] + component_terms(len(PARTS) - 1, far)
            for side in (1, 0):
                pair_copy(it, far, side).start()
        for j in range(1, mates):
            to_mate(wsum_all.at[it, 0], wsum_all.at[it, j], wsum_sems.at[it], j).start()
        for far in (1, 0):
            for side in (1, 0):
                k = far * 2 + side
                pair_copy(it, far, side).wait_recv()
                here = (low + side) % 2 * cores + core
                pair_sum[k] = numh_send[far, here] + pair_recv[it, k]
                if k > 0:
                    chip_copy(it, far, side).start()
        drain(wsum_all.at[it, pl.ds(1, mates - 1)], wsum_sems.at[it, 1])
        w_sum = wsum_all[it, 0]
        for j in range(1, mates):
            w_sum = w_sum + wsum_all[it, j]
        at = lax.broadcasted_iota(jnp.int32, (comps, rank), 1)
        own = lax.broadcasted_iota(jnp.int32, (comps, rank), 0) + scan * comps
        w_sum = jnp.sum(
            jnp.where(at == own, jnp.broadcast_to(w_sum, (comps, rank)), 0.0),
            axis=1,
            keepdims=True,
        )
        total_h = pair_sum[0]
        for far, side in ((0, 1), (1, 0), (1, 1)):
            chip_copy(it, far, side).wait_recv()
            total_h = total_h + numh_recv[it, far * 2 + side - 1]
        h_new = h_now[...] * total_h / w_sum
        if it == ITERS - 1:
            h_out[...] = h_new
        else:
            h_now[...] = h_new
            h_all[it + 1, mine[0], mine[1]] = h_new.astype(BF16)
            send_h(it + 1)

    for g in range(groups):
        frames = pl.ds(g * GROUP, GROUP)
        drain(tile.at[pl.ds(1, SLOTS - 1), :, :, frames], data_sems.at[g, 0])
    for step in range(ITERS + 1):
        for p in range(len(PARTS)):
            drain(w_all[p].at[step, pl.ds(1, SLOTS - 1)], w_sems.at[step, p, 0])
    for step in range(ITERS):
        for far, side in others:
            h_chip(step, far, side).wait_send()
        for far, side in every:
            h_pair(step, far, side).wait_send()
        drain(hsum_all.at[step, pl.ds(1, SLOTS - 1)], hsum_sems.at[step, 0])
        drain(wsum_all.at[step, pl.ds(1, mates - 1)], wsum_sems.at[step, 0])
    for p in range(len(PARTS)):
        drain(num_send[p].at[pl.ds(1, SLOTS - 1)], num_sems.at[ITERS - 1, p, 0])
    for far, side in every:
        pair_copy(ITERS - 1, far, side).wait_send()
    for far, side in others:
        chip_copy(ITERS - 1, far, side).wait_send()


def solution(mesh):
    n_scan = mesh.shape["scan"]
    mates = EX * n_scan

    def local(raw_frames, gain_map, coupling, factor_w, factor_h):
        frames = raw_frames.shape[0]
        rank = factor_w.shape[1]
        comps, pixels = factor_h.shape
        groups = frames // GROUP
        block = pixels // FRAME
        hbm = pl.BlockSpec(memory_space=pl.ANY)
        vmem = pl.BlockSpec(memory_space=pltpu.VMEM)
        dma = pltpu.SemaphoreType.DMA
        return pl.pallas_call(
            functools.partial(kernel, n_scan),
            out_shape=(
                pltpu.VMEM(factor_w.shape, F32),
                pltpu.VMEM(factor_h.shape, F32),
            ),
            in_specs=[hbm] * 5,
            out_specs=(vmem, vmem),
            scratch_shapes=[
                pltpu.VMEM((groups, GROUP * FRAME, LANES), F32),
                pltpu.VMEM((3, FRAME, 8, LANES), F32),
                pltpu.VMEM((FRAME, GROUP, LANES), F32),
                pltpu.VMEM((2, FRAME + 2, GROUP, LANES), F32),
                pltpu.VMEM((2, block, frames, LANES), F32),
                pltpu.VMEM((EY, EX, EZ, block, frames, LANES), DATA),
                pltpu.VMEM((SLOTS, EX, block, frames, LANES), DATA),
                tuple(pltpu.VMEM((ITERS + 1, SLOTS, n, rank), BF16) for _, n in PARTS),
                pltpu.VMEM((frames, rank), F32),
                pltpu.VMEM((FRAME, LANES), F32),
                pltpu.VMEM((FRAME, LANES), F32),
                tuple(pltpu.VMEM((SLOTS, n, rank), F32) for _, n in PARTS),
                tuple(pltpu.VMEM((ITERS, SLOTS, n, rank), F32) for _, n in PARTS),
                pltpu.VMEM((ITERS, rank, EX * pixels), BF16),
                pltpu.VMEM((comps, pixels), F32),
                pltpu.VMEM((ITERS, SLOTS, 1, rank), F32),
                pltpu.VMEM((SLOTS * frames, EX * pixels), BF16),
                pltpu.VMEM((EX, n_scan, comps, pixels), F32),
                pltpu.VMEM((ITERS, mates // 2, comps, pixels), F32),
                pltpu.VMEM((mates // 2, comps, pixels), F32),
                pltpu.VMEM((ITERS, mates // 2 - 1, comps, pixels), F32),
                pltpu.VMEM((ITERS, mates, 1, rank), F32),
                dma((groups + 4,)),
                dma((groups, 3)),
                dma((groups,)),
                dma((ITERS + 1, len(PARTS), 3)),
                dma((ITERS, len(PARTS), 2)),
                dma((ITERS, mates // 2, 2)),
                dma((ITERS, mates // 2, 2)),
                dma((ITERS, 2)),
                dma((ITERS, mates // 2, 2)),
                dma((ITERS, mates // 2, 2)),
                dma((ITERS, 2)),
            ],
            compiler_params=pltpu.CompilerParams(
                collective_id=0, has_side_effects=True, vmem_limit_bytes=58 * 1024 * 1024
            ),
        )(raw_frames.reshape(frames * FRAME, LANES), gain_map, coupling, factor_w, factor_h)

    return jax.shard_map(
        local,
        mesh=mesh,
        in_specs=(
            P(("scan", "pix"), None, None),
            P(),
            P(),
            P(("scan", "pix"), None),
            P("scan", "pix"),
        ),
        out_specs=(P(("scan", "pix"), None), P("scan", "pix")),
        check_vma=False,
    )
```

```python
import functools

import jax
import jax.numpy as jnp
from jax import lax
from jax.experimental import pallas as pl
from jax.experimental.pallas import tpu as pltpu
from jax.sharding import PartitionSpec as P

SWEEPS = 4
ITERS = 2
FRAME = 128
LANES = 128
EY, EX, EZ = 4, 2, 4
SLOTS = EY * EZ
GROUP = 16
ROWS = 64
DATA = jnp.bfloat16
PARTS = tuple((g * GROUP, GROUP) for g in range(3))
UNITS = tuple((g, 0, SLOTS) for g in range(3))
HALF = SLOTS // 2

MESH = pl.DeviceIdType.MESH
F32 = jnp.float32
BF16 = jnp.bfloat16


def kernel(
    n_scan,
    raw_ref,
    gain_ref,
    couple_ref,
    w_ref,
    h_ref,
    w_out,
    h_out,
    raw_v,
    maps,
    scaled,
    field,
    stretch,
    charge,
    tile,
    w_all,
    w_now,
    gain_v,
    couple_v,
    num_send,
    num_recv,
    h_all,
    h_now,
    hsum_all,
    ratio,
    numh_send,
    pair_recv,
    pair_sum,
    numh_recv,
    wsum_all,
    raw_sem,
    data_sems,
    own_sem,
    w_sems,
    num_sems,
    h_sems,
    h_pair_sems,
    hsum_sems,
    pair_sems,
    numh_sems,
    wsum_sems,
):
    rows, rank = w_ref.shape
    comps, pixels = h_ref.shape
    block = pixels // FRAME
    groups = rows // GROUP
    mates = EX * n_scan
    scan = lax.axis_index("scan")
    pix = lax.axis_index("pix")
    my, mx, mz = pix // (EX * EZ), (pix // EZ) % EX, pix % EZ
    cores = n_scan // 2
    low, core = scan // cores, scan % cores
    twin = (core + 1) % cores

    def ahead(slot):
        return (my + slot // EZ) % EY, (mz + slot % EZ) % EZ

    def behind(slot):
        return (my + EY - slot // EZ) % EY, (mz + EZ - slot % EZ) % EZ

    def mate(j):
        other = (mx * n_scan + scan + j) % mates
        return other % n_scan, other // n_scan

    def in_order(go):
        for slot in sorted(range(1, SLOTS), key=lambda d: (min(d // EZ, EY - d // EZ) + min(d % EZ, EZ - d % EZ)), reverse=True):
            go(slot)

    def remote(src, dst, sems, to_scan, y, x, z, part=0):
        return pltpu.make_async_remote_copy(
            src_ref=src,
            dst_ref=dst,
            send_sem=sems.at[0],
            recv_sem=sems.at[1 + part],
            device_id=(to_scan, (y * EX + x) * EZ + z),
            device_id_type=MESH,
        )

    def to_slot(src, dst, sems, where, part=0):
        y, z = where
        return remote(src, dst, sems, scan, y, mx, z, part)

    def to_mate(src, dst, sems, j):
        to_scan, x = mate(j)
        return remote(src, dst, sems, to_scan, my, x, mz)

    def drain(ref, sem):
        pltpu.make_async_copy(ref, ref, sem).wait()

    def fetch(g):
        return pltpu.make_async_copy(
            raw_ref.at[pl.ds(g * GROUP * FRAME, GROUP * FRAME)], raw_v.at[g], raw_sem.at[g]
        )

    small = [
        pltpu.make_async_copy(src, dst, raw_sem.at[groups + i])
        for i, (src, dst) in enumerate(
            ((w_ref, w_now), (h_ref, h_now), (gain_ref, gain_v), (couple_ref, couple_v))
        )
    ]
    for copy in small:
        copy.start()
    for g in range(groups):
        fetch(g).start()

    barrier = pltpu.get_barrier_semaphore()

    def greet(slot, carry):
        y, z = ahead(slot)
        pl.semaphore_signal(
            barrier, inc=1, device_id=(scan, (y * EX + mx) * EZ + z), device_id_type=MESH
        )
        return carry

    lax.fori_loop(1, SLOTS, greet, 0)
    for j in range(1, mates):
        to_scan, x = mate(j)
        pl.semaphore_signal(
            barrier, inc=1, device_id=(to_scan, (my * EX + x) * EZ + mz), device_id_type=MESH
        )

    for copy in small:
        copy.wait()

    def part_rows(p):
        return pl.ds(*PARTS[p])

    def send_w(step, p):
        def go(slot):
            to_slot(
                w_all[p].at[step, 0],
                w_all[p].at[step, slot],
                w_sems.at[step, p],
                ahead(slot),
                slot // HALF,
            ).start()

        in_order(go)

    def halves(u):
        _, start, count = UNITS[u]
        both = ((1, HALF - 1, 0), (HALF, HALF, 1))
        return [h for h in both if start <= h[0] < start + count]

    def wait_w(step, u):
        p = UNITS[u][0]
        for start, count, half in halves(u):
            drain(w_all[p].at[step, pl.ds(start, count)], w_sems.at[step, p, 1 + half])

    def place(far, side, of_core):
        at = (low + side) % 2 * cores + of_core
        return (
            pl.ds(pl.multiple_of(at * comps, comps), comps),
            pl.ds(pl.multiple_of((mx + far) % EX * pixels, pixels), pixels),
        )

    mine = place(0, 0, core)

    def h_chip(step, far, side):
        own = h_all.at[step, mine[0], mine[1]]
        return remote(
            own,
            own,
            h_sems.at[step, far * 2 + side],
            (low + side) % 2 * cores + core,
            my,
            (mx + far) % EX,
            mz,
        )

    def h_pair(step, far, side):
        at = place(far, side, core)
        part = h_all.at[step, at[0], at[1]]
        return remote(
            part, part, h_pair_sems.at[step, far * 2 + side], low * cores + twin, my, mx, mz
        )

    others = ((1, 0), (1, 1), (0, 1))
    every = ((0, 0),) + others

    def send_h(step):
        for far, side in others:
            h_chip(step, far, side).start()
        h_pair(step, 0, 0).start()

    def finish_h(step):
        for far, side in others[::-1]:
            h_chip(step, far, side).wait_recv()
            h_pair(step, far, side).start()
        for far, side in every:
            h_pair(step, far, side).wait_recv()

    for p in range(len(PARTS)):
        w_all[p][0, 0] = w_now[part_rows(p), :].astype(BF16)
    h_all[0, mine[0], mine[1]] = h_now[...].astype(BF16)

    def meet():
        pl.semaphore_wait(barrier, SLOTS - 1 + mates - 1)
        send_h(0)
        for p in range(len(PARTS)):
            send_w(0, p)

    coupling = couple_v[...]
    inverse = 1.0 / (1.0 + 4.0 * coupling)
    gain = gain_v[...]
    for i, value in enumerate((gain, gain * inverse, coupling * inverse)):
        maps[i] = jnp.broadcast_to(value[:, None, :], (FRAME, 8, LANES))

    shape = (block, rows, LANES)
    turn = [lax.broadcasted_iota(jnp.int32, shape, i) for i in range(3)]
    turn = jnp.bitwise_and(107 * turn[0] + 193 * turn[1] + 145 * turn[2], 255)
    factor = 1.0 + (turn.astype(F32) - 127.5) * (2.0**-12)
    stretch[0] = factor
    stretch[1] = 1.0 / factor

    lane = lax.broadcasted_iota(jnp.int32, (ROWS, GROUP, LANES), 2)
    first, last = lane == 0, lane == LANES - 1

    for i in range(2):
        edge = jnp.zeros((GROUP, LANES), F32)
        field[i, 0] = edge
        field[i, FRAME + 1] = edge

    def correct(g, between=None):
        def map_rows(i, at):
            value = maps[i, pl.ds(at, ROWS)]
            return jnp.concatenate([value] * (GROUP // 8), axis=1)

        def start(c, carry):
            at = c * 8
            for i in range(8):
                raw = raw_v[g, pl.ds(at + i, GROUP, stride=FRAME), :]
                tall = [maps[m, at + i] for m in range(2)]
                gain_row, scaled_row = [
                    jnp.concatenate([v] * (GROUP // 8), axis=0) for v in tall
                ]
                field[0, at + i + 1] = raw * gain_row
                scaled[at + i] = raw * scaled_row
            return carry

        lax.fori_loop(0, FRAME // 8, start, 0)
        for s in range(SWEEPS):

            def sweep(c, carry):
                at = c * ROWS
                rows_in = field[s % 2, pl.ds(at, ROWS + 2)]
                mid = rows_in[1:-1]
                left = jnp.where(first, 0.0, pltpu.roll(mid, 1, 2))
                right = jnp.where(last, 0.0, pltpu.roll(mid, LANES - 1, 2))
                value = scaled[pl.ds(at, ROWS)] + map_rows(2, at) * (
                    (rows_in[:-2] + rows_in[2:]) + (left + right)
                )
                if s == SWEEPS - 1:
                    slabs = ROWS // (EX * EZ * block)
                    frames = pl.ds(g * GROUP, GROUP)
                    value = value.reshape(slabs * EX * EZ, block, GROUP, LANES)
                    value = (value * stretch[0, :, frames][None]).astype(charge.dtype)
                    charge[pl.ds(c * slabs, slabs), :, :, :, frames, :] = value.reshape(
                        slabs, EX, EZ, block, GROUP, LANES
                    )
                else:
                    field[(s + 1) % 2, pl.ds(at + 1, ROWS)] = value
                return carry

            lax.fori_loop(0, FRAME // ROWS, sweep, 0)
            if s == 0 and between is not None:
                between()

    def own_copy(g):
        frames = pl.ds(g * GROUP, GROUP)
        return pltpu.make_async_copy(
            charge.at[my, :, mz, :, frames], tile.at[0, :, :, frames], own_sem.at[g]
        )

    for g in range(groups):
        fetch(g).wait()
        correct(g, meet if g == 0 else None)
        own_copy(g).start()
        frames = pl.ds(g * GROUP, GROUP)

        def go(slot):
            y, z = ahead(slot)
            to_slot(
                charge.at[y, :, z, :, frames],
                tile.at[slot, :, :, frames],
                data_sems.at[g],
                (y, z),
                slot // HALF,
            ).start()

        in_order(go)

    wide = EX * pixels
    unit_rows = [count * PARTS[p][1] for p, _, count in UNITS]
    unit_start = [sum(unit_rows[:u]) for u in range(len(UNITS))]

    def pair_copy(it, far, side):
        k = far * 2 + side
        there = (low + side) % 2 * cores + twin
        return remote(
            numh_send.at[far, there],
            pair_recv.at[it, k],
            pair_sems.at[it, k],
            low * cores + twin,
            my,
            mx,
            mz,
        )

    def chip_copy(it, far, side):
        k = far * 2 + side
        return remote(
            pair_sum.at[k],
            numh_recv.at[it, k - 1],
            numh_sems.at[it, k],
            (low + side) % 2 * cores + core,
            my,
            (mx + far) % EX,
            mz,
        )
    wide = EX * pixels

    def wait_data(u):
        p, start, _ = UNITS[u]
        first_frame, count = PARTS[p]
        for g in range(first_frame // GROUP, (first_frame + count) // GROUP):
            frames = pl.ds(g * GROUP, GROUP)
            if start == 0:
                own_copy(g).wait()
            for at, n, half in halves(u):
                drain(tile.at[pl.ds(at, n), :, :, frames], data_sems.at[g, 1 + half])

    def unit_w(step, u):
        p, start, count = UNITS[u]
        return w_all[p][step, pl.ds(start, count)].reshape(unit_rows[u], rank)

    def ratios(step_w, step_h, u):
        p, start, count = UNITS[u]
        slots = pl.ds(start, count)
        product = jnp.dot(unit_w(step_w, u), h_all[step_h], preferred_element_type=F32)
        parts = []
        for x in range(EX):
            for k in range(block):
                at = (x * block + k) * LANES
                data = tile[slots, x, k, part_rows(p)].astype(F32) * stretch[1, k, part_rows(p)][None]
                data = data.reshape(unit_rows[u], LANES)
                parts.append((data / product[:, at : at + LANES]).astype(BF16))
        return jnp.concatenate(parts, axis=1)

    for it in range(ITERS):
        finish_h(it)
        for u, (p, start, count) in enumerate(UNITS):
            if it == 0:
                wait_w(0, u)
                wait_data(u)
            elif start == 0:
                drain(num_send[p].at[pl.ds(1, SLOTS - 1)], num_sems.at[it - 1, p, 0])
            terms = ratios(it, it, u)
            if u == 0:
                terms = jnp.concatenate([terms, jnp.ones((16, wide), BF16)], axis=0)
            terms = lax.dot_general(
                terms, h_all[it], (((1,), (1,)), ((), ())), preferred_element_type=F32
            )
            num_send[p][pl.ds(start, count)] = terms[: unit_rows[u]].reshape(
                count, PARTS[p][1], rank
            )

            def go(slot):
                to_slot(
                    num_send[p].at[slot],
                    num_recv[p].at[it, slot],
                    num_sems.at[it, p],
                    behind(slot),
                ).start()

            in_order(go)
            if u == 0:
                hsum_all[it, 0] = terms[unit_rows[u] : unit_rows[u] + 1]

                def share(slot, carry):
                    to_slot(
                        hsum_all.at[it, 0], hsum_all.at[it, slot], hsum_sems.at[it], ahead(slot)
                    ).start()
                    return carry

                lax.fori_loop(1, SLOTS, share, 0)

        drain(hsum_all.at[it, pl.ds(1, SLOTS - 1)], hsum_sems.at[it, 1])
        h_sum = hsum_all[it, 0]
        for slot in range(1, SLOTS):
            h_sum = h_sum + hsum_all[it, slot]
        for p in range(len(PARTS)):
            drain(num_recv[p].at[it, pl.ds(1, SLOTS - 1)], num_sems.at[it, p, 1])

            def add(slot, total):
                return total + num_recv[p][it, slot]

            total = lax.fori_loop(1, SLOTS, add, num_send[p][0], unroll=True)
            w_new = w_now[part_rows(p), :] * total / h_sum
            w_now[part_rows(p), :] = w_new
            w_all[p][it + 1, 0] = w_new.astype(BF16)
            send_w(it + 1, p)
        if it == ITERS - 1:
            w_out[...] = w_now[...]

        if it > 0:
            for far, side in every:
                pair_copy(it - 1, far, side).wait_send()
            for far, side in others:
                chip_copy(it - 1, far, side).wait_send()

        def component_terms(p, far):
            units = [u for u in range(len(UNITS)) if UNITS[u][0] == p]
            count = SLOTS * PARTS[p][1]
            x = (mx + far) % EX
            return lax.dot_general(
                w_all[p][it + 1].reshape(count, rank),
                ratio[
                    pl.ds(unit_start[units[0]], count),
                    pl.ds(pl.multiple_of(x * pixels, pixels), pixels),
                ],
                (((0,), (0,)), ((), ())),
                preferred_element_type=F32,
            ).reshape(n_scan, comps, pixels)

        w_sum = jnp.zeros((1, rank), F32)
        for u in range(len(UNITS)):
            wait_w(it + 1, u)
            ratio[pl.ds(unit_start[u], unit_rows[u]), :] = ratios(it + 1, it, u)
            w_sum = w_sum + jnp.sum(unit_w(it + 1, u).astype(F32), axis=0, keepdims=True)
            p = UNITS[u][0]
            if p < len(PARTS) - 1 and UNITS[u + 1][0] > p:
                for far in (1, 0):
                    terms = component_terms(p, far)
                    numh_send[far] = terms if p == 0 else numh_send[far] + terms
        wsum_all[it, 0] = w_sum
        for far in (1, 0):
            numh_send[far] = numh_send[far] + component_terms(len(PARTS) - 1, far)
            for side in (1, 0):
                pair_copy(it, far, side).start()
        for j in range(1, mates):
            to_mate(wsum_all.at[it, 0], wsum_all.at[it, j], wsum_sems.at[it], j).start()
        for far in (1, 0):
            for side in (1, 0):
                k = far * 2 + side
                pair_copy(it, far, side).wait_recv()
                here = (low + side) % 2 * cores + core
                pair_sum[k] = numh_send[far, here] + pair_recv[it, k]
                if k > 0:
                    chip_copy(it, far, side).start()
        drain(wsum_all.at[it, pl.ds(1, mates - 1)], wsum_sems.at[it, 1])
        w_sum = wsum_all[it, 0]
        for j in range(1, mates):
            w_sum = w_sum + wsum_all[it, j]
        at = lax.broadcasted_iota(jnp.int32, (comps, rank), 1)
        own = lax.broadcasted_iota(jnp.int32, (comps, rank), 0) + scan * comps
        w_sum = jnp.sum(
            jnp.where(at == own, jnp.broadcast_to(w_sum, (comps, rank)), 0.0),
            axis=1,
            keepdims=True,
        )
        total_h = pair_sum[0]
        for far, side in ((0, 1), (1, 0), (1, 1)):
            chip_copy(it, far, side).wait_recv()
            total_h = total_h + numh_recv[it, far * 2 + side - 1]
        h_new = h_now[...] * total_h / w_sum
        if it == ITERS - 1:
            h_out[...] = h_new
        else:
            h_now[...] = h_new
            h_all[it + 1, mine[0], mine[1]] = h_new.astype(BF16)
            send_h(it + 1)

    for g in range(groups):
        frames = pl.ds(g * GROUP, GROUP)
        drain(tile.at[pl.ds(1, SLOTS - 1), :, :, frames], data_sems.at[g, 0])
    for step in range(ITERS + 1):
        for p in range(len(PARTS)):
            drain(w_all[p].at[step, pl.ds(1, SLOTS - 1)], w_sems.at[step, p, 0])
    for step in range(ITERS):
        for far, side in others:
            h_chip(step, far, side).wait_send()
        for far, side in every:
            h_pair(step, far, side).wait_send()
        drain(hsum_all.at[step, pl.ds(1, SLOTS - 1)], hsum_sems.at[step, 0])
        drain(wsum_all.at[step, pl.ds(1, mates - 1)], wsum_sems.at[step, 0])
    for p in range(len(PARTS)):
        drain(num_send[p].at[pl.ds(1, SLOTS - 1)], num_sems.at[ITERS - 1, p, 0])
    for far, side in every:
        pair_copy(ITERS - 1, far, side).wait_send()
    for far, side in others:
        chip_copy(ITERS - 1, far, side).wait_send()


def solution(mesh):
    n_scan = mesh.shape["scan"]
    mates = EX * n_scan

    def local(raw_frames, gain_map, coupling, factor_w, factor_h):
        frames = raw_frames.shape[0]
        rank = factor_w.shape[1]
        comps, pixels = factor_h.shape
        groups = frames // GROUP
        block = pixels // FRAME
        hbm = pl.BlockSpec(memory_space=pl.ANY)
        vmem = pl.BlockSpec(memory_space=pltpu.VMEM)
        dma = pltpu.SemaphoreType.DMA
        return pl.pallas_call(
            functools.partial(kernel, n_scan),
            out_shape=(
                pltpu.VMEM(factor_w.shape, F32),
                pltpu.VMEM(factor_h.shape, F32),
            ),
            in_specs=[hbm] * 5,
            out_specs=(vmem, vmem),
            scratch_shapes=[
                pltpu.VMEM((groups, GROUP * FRAME, LANES), F32),
                pltpu.VMEM((3, FRAME, 8, LANES), F32),
                pltpu.VMEM((FRAME, GROUP, LANES), F32),
                pltpu.VMEM((2, FRAME + 2, GROUP, LANES), F32),
                pltpu.VMEM((2, block, frames, LANES), F32),
                pltpu.VMEM((EY, EX, EZ, block, frames, LANES), DATA),
                pltpu.VMEM((SLOTS, EX, block, frames, LANES), DATA),
                tuple(pltpu.VMEM((ITERS + 1, SLOTS, n, rank), BF16) for _, n in PARTS),
                pltpu.VMEM((frames, rank), F32),
                pltpu.VMEM((FRAME, LANES), F32),
                pltpu.VMEM((FRAME, LANES), F32),
                tuple(pltpu.VMEM((SLOTS, n, rank), F32) for _, n in PARTS),
                tuple(pltpu.VMEM((ITERS, SLOTS, n, rank), F32) for _, n in PARTS),
                pltpu.VMEM((ITERS, rank, EX * pixels), BF16),
                pltpu.VMEM((comps, pixels), F32),
                pltpu.VMEM((ITERS, SLOTS, 1, rank), F32),
                pltpu.VMEM((SLOTS * frames, EX * pixels), BF16),
                pltpu.VMEM((EX, n_scan, comps, pixels), F32),
                pltpu.VMEM((ITERS, mates // 2, comps, pixels), F32),
                pltpu.VMEM((mates // 2, comps, pixels), F32),
                pltpu.VMEM((ITERS, mates // 2 - 1, comps, pixels), F32),
                pltpu.VMEM((ITERS, mates, 1, rank), F32),
                dma((groups + 4,)),
                dma((groups, 3)),
                dma((groups,)),
                dma((ITERS + 1, len(PARTS), 3)),
                dma((ITERS, len(PARTS), 2)),
                dma((ITERS, mates // 2, 2)),
                dma((ITERS, mates // 2, 2)),
                dma((ITERS, 2)),
                dma((ITERS, mates // 2, 2)),
                dma((ITERS, mates // 2, 2)),
                dma((ITERS, 2)),
            ],
            compiler_params=pltpu.CompilerParams(
                collective_id=0, has_side_effects=True, vmem_limit_bytes=58 * 1024 * 1024
            ),
        )(raw_frames.reshape(frames * FRAME, LANES), gain_map, coupling, factor_w, factor_h)

    return jax.shard_map(
        local,
        mesh=mesh,
        in_specs=(
            P(("scan", "pix"), None, None),
            P(),
            P(),
            P(("scan", "pix"), None),
            P("scan", "pix"),
        ),
        out_specs=(P(("scan", "pix"), None), P("scan", "pix")),
        check_vma=False,
    )
```
